128 devices in a mesh: range: 128 (over z, x, y, core).
Axes of the slice: x: 4, y: 4, z: 4, core: 2. Of those that a mesh axis runs over, the one named last changes fastest.
Arguments:
- child_in: bfloat16 [4096, 128, 128], P('range'), may hold values from -6 to 6
- cotangent: bfloat16 [512, 128, 128], P('range'), may hold values from -6 to 6
- child_of: int32 [512, 8], P('range'), may hold values from 0 to 4095, as said below
- neighbours: int32 [512, 27], P('range'), may hold values from -1 to 511, as said below
- down_w: bfloat16 [8, 128, 128], replicated, may hold values from -0.1875 to 0.1875
- first_w: bfloat16 [27, 128, 128], replicated, may hold values from -0.109375 to 0.109375
- second_w: bfloat16 [27, 128, 128], replicated, may hold values from -0.109375 to 0.109375
Outputs:
- section_out: bfloat16 [512, 128, 128], P('range')
- child_grad: bfloat16 [4096, 128, 128], P('range')
- down_grad: float32 [8, 128, 128], replicated
- first_grad: float32 [27, 128, 128], replicated
- second_grad: float32 [27, 128, 128], replicated
The draws below stay inside these ranges and needn't reach their ends.
Inputs may be any that keep to these rules, and one draw needn't show every extreme that they name: `neighbours`: the coarse blocks fill a grid of 2 x 2 x 128 blocks; indices 4l to 4l + 3 are the four blocks of layer l (third block coordinate l) in some order. Entry k names the block at block offset d_k = (k // 9 - 1, k // 3 % 3 - 1, k % 3 - 1), -1 where it lies outside the grid, so the relation is symmetric. `child_of`: the fine blocks fill a grid of 4 x 4 x 2 * 128 blocks; the fine block at octant 4a + 2c + e of the coarse block at (i, j, l) sits at (2i + a, 2j + c, 2l + e). Every fine block appears once, and the children of a coarse block held by device d have indices d * 32 to (d + 1) * 32 - 1.
All inputs are finite; a program needn't handle non-finite values.
Results may differ from the reference program's by a relative error of at most 0.0055.
Values may be sent and summed in bfloat16 or wider, within the bound.
A program may use at most 128 MiB of HBM per device.

```python
import math
import jax
import jax.numpy as jnp
from jax import lax

C = 128
PX = 4
PY = 4
PZ = 8
ZD = 1
CH_DEV = 32
LAYERS = 128
PBLK = 512
CBLK = 4096
N_RANGE = 128


def layer_slots(key):
    layer_keys = jax.random.split(jax.random.fold_in(key, 7), LAYERS)
    cross_slot = jax.vmap(lambda one_key: jax.random.permutation(one_key, 4))(layer_keys).astype(jnp.int32)
    cross_place = jnp.argsort(cross_slot, axis=1, stable=True).astype(jnp.int32)
    block_ids = jnp.arange(PBLK, dtype=jnp.int32)
    layer_of = block_ids // 4
    place_of = cross_place[layer_of, block_ids % 4]
    return (cross_slot, layer_of, place_of // 2, place_of % 2)


def draw_neighbours(key, part):
    cross_slot, layer_of, grid_x, grid_y = layer_slots(key)
    offsets = jnp.arange(27, dtype=jnp.int32)
    shift_x = offsets // 9 - 1
    shift_y = offsets // 3 % 3 - 1
    shift_z = offsets % 3 - 1
    near_x = grid_x[:, None] + shift_x[None, :]
    near_y = grid_y[:, None] + shift_y[None, :]
    near_layer = layer_of[:, None] + shift_z[None, :]
    inside = (near_x >= 0) & (near_x < 2) & (near_y >= 0) & (near_y < 2) & (near_layer >= 0) & (near_layer < LAYERS)
    layer_safe = jnp.clip(near_layer, 0, LAYERS - 1)
    place_safe = jnp.clip(near_x, 0, 1) * 2 + jnp.clip(near_y, 0, 1)
    chosen = 4 * layer_safe + cross_slot[layer_safe, place_safe]
    return jnp.where(inside, chosen, -1).astype(jnp.int32)


def draw_child_of(key, part):
    cross_slot, layer_of, grid_x, grid_y = layer_slots(key)
    octants = jnp.arange(8, dtype=jnp.int32)
    child_x = 2 * grid_x[:, None] + octants[None, :] // 4
    child_y = 2 * grid_y[:, None] + octants[None, :] // 2 % 2
    child_z = 2 * layer_of[:, None] + octants[None, :] % 2
    owner_device = child_z // (2 * ZD)
    local_pos = (child_z - owner_device * 2 * ZD) * 16 + child_x * 4 + child_y
    device_keys = jax.random.split(jax.random.fold_in(key, 13), N_RANGE)
    device_perms = jax.vmap(lambda one_key: jax.random.permutation(one_key, CH_DEV))(device_keys).astype(jnp.int32)
    return (owner_device * CH_DEV + device_perms[owner_device, local_pos]).astype(jnp.int32)


def levels(own_key, extent, shards, smallest, top_value):
    level, own = 1.0, jax.random.fold_in(own_key, 6)
    for axis_at, parts in shards:
        heights = jnp.exp(jax.random.uniform(jax.random.fold_in(own, axis_at), (parts,), jnp.float32, smallest / len(shards), top_value / len(shards)))
        level = level * jnp.repeat(heights, extent[axis_at] // parts).reshape([-1 if axis == axis_at else 1 for axis in range(len(extent))])
    return level


def noise(stream_key, extent, deviation, reach, cuts=(), kind=jnp.bfloat16):
    values = deviation * jax.random.normal(stream_key, extent, jnp.float32)
    if cuts:
        values = values * levels(stream_key, extent, cuts, -0.22, 0.18)
    return jnp.clip(values, -reach, reach).astype(kind)


def setup_inputs(seed: int = 0) -> dict:
    keys = jax.random.split(jax.random.key(seed), 8)
    child_in = noise(keys[0], (CBLK, PX * PY * PZ, C), 1.0, 6.0, ((0, 128),))
    cotangent = noise(keys[1], (PBLK, PX * PY * PZ, C), 1.0, 6.0, ((0, 128),))
    child_of = draw_child_of(jax.random.fold_in(keys[7], 71), 0)
    neighbours = draw_neighbours(jax.random.fold_in(keys[7], 71), 0)
    down_w = noise(keys[4], (8, C, C), (8 * C) ** -0.5, 0.1875)
    first_w = noise(keys[5], (27, C, C), (27 * C) ** -0.5, 0.109375)
    second_w = noise(keys[6], (27, C, C), (27 * C) ** -0.5, 0.109375)
    return dict(child_in=child_in, cotangent=cotangent, child_of=child_of, neighbours=neighbours, down_w=down_w, first_w=first_w, second_w=second_w)


def build_cols(feature_table, block_rows):
    block_count = block_rows.shape[0]
    channels = feature_table.shape[-1]
    gathered = feature_table[block_rows]
    gathered = gathered.reshape(block_count, 3, 3, 3, PX, PY, PZ, channels).transpose(0, 1, 4, 2, 5, 3, 6, 7)
    gathered = gathered.reshape(block_count, 3 * PX, 3 * PY, 3 * PZ, channels)
    padded = gathered[:, PX - 1:2 * PX + 1, PY - 1:2 * PY + 1, PZ - 1:2 * PZ + 1]
    column_parts = [padded[:, step_x:step_x + PX, step_y:step_y + PY, step_z:step_z + PZ] for step_x in range(3) for step_y in range(3) for step_z in range(3)]
    return jnp.stack(column_parts, axis=4).reshape(block_count * PX * PY * PZ, 27 * channels)

def child_cols(feature_table, block_rows):
    block_count = block_rows.shape[0]
    channels = feature_table.shape[-1]
    gathered = feature_table[block_rows].reshape(block_count, 2, 2, 2, PX, PY, PZ, channels).transpose(0, 1, 4, 2, 5, 3, 6, 7)
    gathered = gathered.reshape(block_count, PX, 2, PY, 2, PZ, 2, channels).transpose(0, 1, 3, 5, 2, 4, 6, 7)
    return gathered.reshape(block_count * PX * PY * PZ, 8 * channels)

def child_split(columns, block_count):
    channels = columns.shape[-1] // 8
    spread = columns.reshape(block_count, PX, PY, PZ, 2, 2, 2, channels).transpose(0, 1, 4, 2, 5, 3, 6, 7)
    spread = spread.reshape(block_count, 2, PX, 2, PY, 2, PZ, channels).transpose(0, 1, 3, 5, 2, 4, 6, 7)
    return spread.reshape(block_count * 8, PX * PY * PZ, channels)

def flipped(weight):
    return jnp.flip(weight, 0).transpose(0, 2, 1).reshape(-1, weight.shape[-1])

def reference(child_in, cotangent, child_of, neighbours, down_w, first_w, second_w):
    channels = child_in.shape[-1]
    voxels = PX * PY * PZ
    groups = N_RANGE
    group_size = PBLK // groups
    child_rows = child_of.astype(jnp.int32).reshape(groups, group_size, 8)
    near_rows = jnp.where(neighbours < 0, PBLK, neighbours).astype(jnp.int32).reshape(groups, group_size, 27)
    zero_block = jnp.zeros((1, voxels, channels), jnp.bfloat16)
    down_flat = down_w.reshape(8 * channels, channels)

    def widen(field):
        return jnp.concatenate([field.reshape(PBLK, voxels, channels), zero_block], 0)

    def down_step(block_rows):
        return jnp.dot(child_cols(child_in, block_rows), down_flat, preferred_element_type=jnp.float32).astype(jnp.bfloat16)
    hidden = lax.map(down_step, child_rows)
    hidden_table = widen(hidden)

    def conv_map(feature_table, weight):
        return lax.map(lambda block_rows: jnp.dot(build_cols(feature_table, block_rows), weight, preferred_element_type=jnp.float32), near_rows)
    pre_act = conv_map(hidden_table, first_w.reshape(-1, channels))
    activated = jax.nn.silu(pre_act).astype(jnp.bfloat16)
    act_table = widen(activated)
    section_out = (hidden.astype(jnp.float32) + conv_map(act_table, second_w.reshape(-1, channels))).astype(jnp.bfloat16)
    grad_rows = cotangent.reshape(groups, group_size * voxels, channels)
    back_act = conv_map(widen(cotangent), flipped(second_w))
    sigmoid_pre = jax.nn.sigmoid(pre_act)
    d_pre = (back_act * sigmoid_pre * (1.0 + pre_act * (1.0 - sigmoid_pre))).astype(jnp.bfloat16)
    d_hidden = (grad_rows.astype(jnp.float32) + conv_map(widen(d_pre), flipped(first_w))).astype(jnp.bfloat16)

    def weight_term(feature_table):

        def inner(item_pair):
            return jnp.dot(build_cols(feature_table, item_pair[0]).T, item_pair[1], preferred_element_type=jnp.float32)
        return inner
    raw_first = lax.optimization_barrier(jnp.sum(lax.map(weight_term(hidden_table), (near_rows, d_pre)), 0))
    raw_second = lax.optimization_barrier(jnp.sum(lax.map(weight_term(act_table), (near_rows, grad_rows)), 0))

    def child_step(item_pair):
        columns = child_cols(child_in, item_pair[0])
        term = jnp.dot(columns.T, item_pair[1], preferred_element_type=jnp.float32)
        back_cols = jnp.dot(item_pair[1], down_flat.T, preferred_element_type=jnp.float32).astype(jnp.bfloat16)
        return (term, child_split(back_cols, group_size))
    terms, pieces = lax.map(child_step, (child_rows, d_hidden))
    raw_down = lax.optimization_barrier(jnp.sum(terms, 0))
    child_grad = jnp.zeros((CBLK, voxels, channels), jnp.bfloat16).at[child_rows.reshape(-1)].set(pieces.reshape(-1, voxels, channels))
    raw_grads = jnp.concatenate([raw_down.reshape(8, channels, channels), raw_first.reshape(27, channels, channels), raw_second.reshape(27, channels, channels)], 0)
    grad_total = jnp.sqrt(jnp.sum(raw_grads * raw_grads))
    factor = jnp.minimum(jnp.float32(1.0), jnp.float32(channels * math.sqrt(62.0)) / grad_total)
    clipped = raw_grads * factor
    return (section_out.reshape(PBLK, voxels, channels), child_grad, clipped[:8], clipped[8:35], clipped[35:62])
```

```python
import math

import jax
import jax.numpy as jnp
from jax import lax
from jax.sharding import PartitionSpec as P

PX = 4
PY = 4
PZ = 8


def to_grid(slots):
    channels = slots.shape[-1]
    g = slots.reshape(2, 2, PX, PY, PZ, channels).transpose(0, 2, 1, 3, 4, 5)
    return g.reshape(2 * PX, 2 * PY, PZ, channels)


def from_grid(grid):
    channels = grid.shape[-1]
    g = grid.reshape(2, PX, 2, PY, PZ, channels).transpose(0, 2, 1, 3, 4, 5)
    return g.reshape(4, PX * PY * PZ, channels)


def padded(grid):
    count = lax.axis_size("range")
    forward = [(i, i + 1) for i in range(count - 1)]
    backward = [(i + 1, i) for i in range(count - 1)]
    low = lax.ppermute(grid[:, :, PZ - 1 :], "range", forward)
    high = lax.ppermute(grid[:, :, :1], "range", backward)
    wide = jnp.concatenate([low, grid, high], axis=2)
    return jnp.pad(wide, ((1, 1), (1, 1), (0, 0), (0, 0)))


def columns(pad):
    channels = pad.shape[-1]
    parts = [
        pad[sx : sx + 2 * PX, sy : sy + 2 * PY, sz : sz + PZ]
        for sx in range(3)
        for sy in range(3)
        for sz in range(3)
    ]
    return jnp.concatenate(parts, axis=-1).reshape(-1, 27 * channels)


def reversed_kernel(weights):
    return jnp.flip(weights, 0).transpose(0, 2, 1)


def on_device(child_in, cotangent, child_of, neighbours, down_w, first_w, second_w):
    channels = child_in.shape[-1]
    kids_dev = child_in.shape[0]
    own_rank = lax.axis_index("range")
    f32 = jnp.float32
    bf16 = jnp.bfloat16

    slot_of = 2 * (neighbours[:, 4] >= 0).astype(jnp.int32) + (neighbours[:, 10] >= 0).astype(jnp.int32)
    match = slot_of[None, :] == jnp.arange(4, dtype=jnp.int32)[:, None]
    block_at = jnp.sum(jnp.where(match, jnp.arange(4, dtype=jnp.int32)[None, :], 0), axis=1)
    child_rows = child_of - own_rank * kids_dev
    fine_idx = child_rows[block_at].reshape(-1)
    inverse = jnp.zeros((kids_dev,), jnp.int32).at[fine_idx].set(jnp.arange(kids_dev, dtype=jnp.int32))

    fine = child_in[fine_idx].reshape(2, 2, 2, 2, 2, 2, 2, 2, 2, 4, 2, channels)
    patches = fine.transpose(0, 2, 5, 1, 3, 7, 4, 9, 6, 8, 10, 11).reshape(512, 8 * channels)
    down_flat = down_w.reshape(8 * channels, channels)
    hidden = jnp.dot(patches, down_flat, preferred_element_type=f32).astype(bf16)
    hidden_grid = hidden.reshape(2 * PX, 2 * PY, PZ, channels)

    hidden_cols = columns(padded(hidden_grid))
    pre_act = jnp.dot(hidden_cols, first_w.reshape(-1, channels), preferred_element_type=f32)
    activated = jax.nn.silu(pre_act).astype(bf16)
    act_cols = columns(padded(activated.reshape(2 * PX, 2 * PY, PZ, channels)))
    section = (
        hidden.astype(f32) + jnp.dot(act_cols, second_w.reshape(-1, channels), preferred_element_type=f32)
    ).astype(bf16)

    cot_grid = to_grid(cotangent[block_at])
    cot_rows = cot_grid.reshape(-1, channels)
    cot_cols = columns(padded(cot_grid))
    back_act = jnp.dot(cot_cols, reversed_kernel(second_w).reshape(-1, channels), preferred_element_type=f32)
    sigmoid_pre = jax.nn.sigmoid(pre_act)
    d_pre = (back_act * sigmoid_pre * (1.0 + pre_act * (1.0 - sigmoid_pre))).astype(bf16)
    d_pre_cols = columns(padded(d_pre.reshape(2 * PX, 2 * PY, PZ, channels)))
    d_hidden = (
        cot_rows.astype(f32)
        + jnp.dot(d_pre_cols, reversed_kernel(first_w).reshape(-1, channels), preferred_element_type=f32)
    ).astype(bf16)

    contract_rows = (((0,), (0,)), ((), ()))
    raw_first = lax.dot_general(hidden_cols, d_pre, contract_rows, preferred_element_type=f32)
    raw_second = lax.dot_general(act_cols, cot_rows, contract_rows, preferred_element_type=f32)
    raw_down = lax.dot_general(patches, d_hidden, contract_rows, preferred_element_type=f32)

    back = jnp.dot(d_hidden, down_flat.T, preferred_element_type=f32).astype(bf16)
    back = back.reshape(2, 2, 2, 2, 2, 2, 2, 4, 2, 2, 2, channels)
    back = back.transpose(0, 3, 1, 4, 6, 2, 8, 5, 9, 7, 10, 11).reshape(kids_dev, PX * PY * PZ, channels)
    child_grad = back[inverse]

    raw_grads = jnp.concatenate(
        [
            raw_down.reshape(8, channels, channels),
            raw_first.reshape(27, channels, channels),
            raw_second.reshape(27, channels, channels),
        ],
        0,
    )
    limit = jnp.float32(channels * math.sqrt(62.0))
    summed = lax.psum(raw_grads, "range")
    grad_total = jnp.sqrt(jnp.sum(summed * summed))
    clipped = summed * jnp.minimum(jnp.float32(1.0), limit / grad_total)
    section_out = from_grid(section.reshape(2 * PX, 2 * PY, PZ, channels))[slot_of]
    return (section_out, child_grad, clipped[:8], clipped[8:35], clipped[35:62])


def solution(mesh):
    in_specs = (
        P("range", None, None),
        P("range", None, None),
        P("range", None),
        P("range", None),
        P(),
        P(),
        P(),
    )
    out_specs = (P("range", None, None), P("range", None, None), P(), P(), P())
    return jax.shard_map(
        on_device, mesh=mesh, in_specs=in_specs, out_specs=out_specs, check_vma=False
    )
```

```python
import math

import jax
import jax.numpy as jnp
from jax import lax
from jax.sharding import PartitionSpec as P

PX = 4
PY = 4
PZ = 8


def to_grid(slots):
    channels = slots.shape[-1]
    g = slots.reshape(2, 2, PX, PY, PZ, channels).transpose(0, 2, 1, 3, 4, 5)
    return g.reshape(2 * PX, 2 * PY, PZ, channels)


def from_grid(grid):
    channels = grid.shape[-1]
    g = grid.reshape(2, PX, 2, PY, PZ, channels).transpose(0, 2, 1, 3, 4, 5)
    return g.reshape(4, PX * PY * PZ, channels)


def padded(grid):
    count = lax.axis_size("range")
    forward = [(i, i + 1) for i in range(count - 1)]
    backward = [(i + 1, i) for i in range(count - 1)]
    low = lax.ppermute(grid[:, :, PZ - 1 :], "range", forward)
    high = lax.ppermute(grid[:, :, :1], "range", backward)
    wide = jnp.concatenate([low, grid, high], axis=2)
    return jnp.pad(wide, ((1, 1), (1, 1), (0, 0), (0, 0)))


def columns(pad):
    channels = pad.shape[-1]
    parts = [
        pad[sx : sx + 2 * PX, sy : sy + 2 * PY, sz : sz + PZ]
        for sx in range(3)
        for sy in range(3)
        for sz in range(3)
    ]
    return jnp.concatenate(parts, axis=-1).reshape(-1, 27 * channels)


AXIS_SHIFT = {"y": 1, "x": 3, "z": 5}
PART_ORDERS = (("y", "x", "z"), ("x", "z", "y"), ("z", "y", "x"))


def coordinate(index, shift):
    return (index >> shift) & 3


def partner(index, shift, stage):
    c = (index >> shift) & 3
    other = c ^ 1 if stage == 0 else 3 - c
    return index + ((other - c) << shift)


def keep_bit(c, stage):
    if stage == 0:
        return ((c == 1) | (c == 2)).astype(jnp.int32)
    return (c >= 2).astype(jnp.int32)


def exchange_steps(order):
    return [(AXIS_SHIFT[axis], stage) for axis in order for stage in (0, 1)]


def split_halves(y, bit):
    h = y.shape[0] // 2
    keep = lax.dynamic_slice_in_dim(y, bit * h, h, 0)
    send = lax.dynamic_slice_in_dim(y, (1 - bit) * h, h, 0)
    return keep, send


def join_halves(y, got, bit):
    h = y.shape[0]
    full = jnp.zeros((2 * h,) + y.shape[1:], y.dtype)
    full = lax.dynamic_update_slice_in_dim(full, y, bit * h, 0)
    return lax.dynamic_update_slice_in_dim(full, got, (1 - bit) * h, 0)


def torus_psum(flat):
    count = lax.axis_size("range")
    index = lax.axis_index("range")
    core_perm = [(i, i ^ 1) for i in range(count)]
    core_bit = index & 1
    keep, send = split_halves(flat, core_bit)
    y = keep + lax.ppermute(send, "range", core_perm)
    parts = jnp.split(y, len(PART_ORDERS), 0)
    reduced = []
    for part, order in zip(parts, PART_ORDERS):
        for shift, stage in exchange_steps(order):
            perm = [(i, partner(i, shift, stage)) for i in range(count)]
            bit = keep_bit(coordinate(index, shift), stage)
            keep, send = split_halves(part, bit)
            part = keep + lax.ppermute(send, "range", perm)
        reduced.append(part)
    gathered = []
    for part, order in zip(reduced, PART_ORDERS):
        for shift, stage in reversed(exchange_steps(order)):
            perm = [(i, partner(i, shift, stage)) for i in range(count)]
            bit = keep_bit(coordinate(index, shift), stage)
            part = join_halves(part, lax.ppermute(part, "range", perm), bit)
        gathered.append(part)
    y = jnp.concatenate(gathered, 0)
    return join_halves(y, lax.ppermute(y, "range", core_perm), core_bit)


def reversed_kernel(weights):
    return jnp.flip(weights, 0).transpose(0, 2, 1)


def on_device(child_in, cotangent, child_of, neighbours, down_w, first_w, second_w):
    channels = child_in.shape[-1]
    kids_dev = child_in.shape[0]
    own_rank = lax.axis_index("range")
    f32 = jnp.float32
    bf16 = jnp.bfloat16

    slot_of = 2 * (neighbours[:, 4] >= 0).astype(jnp.int32) + (neighbours[:, 10] >= 0).astype(jnp.int32)
    match = slot_of[None, :] == jnp.arange(4, dtype=jnp.int32)[:, None]
    block_at = jnp.sum(jnp.where(match, jnp.arange(4, dtype=jnp.int32)[None, :], 0), axis=1)
    child_rows = child_of - own_rank * kids_dev
    fine_idx = child_rows[block_at].reshape(-1)
    inverse = jnp.zeros((kids_dev,), jnp.int32).at[fine_idx].set(jnp.arange(kids_dev, dtype=jnp.int32))

    fine = child_in[fine_idx].reshape(2, 2, 2, 2, 2, 2, 2, 2, 2, 4, 2, channels)
    patches = fine.transpose(0, 2, 5, 1, 3, 7, 4, 9, 6, 8, 10, 11).reshape(512, 8 * channels)
    down_flat = down_w.reshape(8 * channels, channels)
    hidden = jnp.dot(patches, down_flat, preferred_element_type=f32).astype(bf16)
    hidden_grid = hidden.reshape(2 * PX, 2 * PY, PZ, channels)

    hidden_cols = columns(padded(hidden_grid))
    pre_act = jnp.dot(hidden_cols, first_w.reshape(-1, channels), preferred_element_type=f32)
    activated = jax.nn.silu(pre_act).astype(bf16)
    act_cols = columns(padded(activated.reshape(2 * PX, 2 * PY, PZ, channels)))
    section = (
        hidden.astype(f32) + jnp.dot(act_cols, second_w.reshape(-1, channels), preferred_element_type=f32)
    ).astype(bf16)

    cot_grid = to_grid(cotangent[block_at])
    cot_rows = cot_grid.reshape(-1, channels)
    cot_cols = columns(padded(cot_grid))
    back_act = jnp.dot(cot_cols, reversed_kernel(second_w).reshape(-1, channels), preferred_element_type=f32)
    sigmoid_pre = jax.nn.sigmoid(pre_act)
    d_pre = (back_act * sigmoid_pre * (1.0 + pre_act * (1.0 - sigmoid_pre))).astype(bf16)
    d_pre_cols = columns(padded(d_pre.reshape(2 * PX, 2 * PY, PZ, channels)))
    d_hidden = (
        cot_rows.astype(f32)
        + jnp.dot(d_pre_cols, reversed_kernel(first_w).reshape(-1, channels), preferred_element_type=f32)
    ).astype(bf16)

    contract_rows = (((0,), (0,)), ((), ()))
    raw_first = lax.dot_general(hidden_cols, d_pre, contract_rows, preferred_element_type=f32)
    raw_second = lax.dot_general(act_cols, cot_rows, contract_rows, preferred_element_type=f32)
    raw_down = lax.dot_general(patches, d_hidden, contract_rows, preferred_element_type=f32)

    back = jnp.dot(d_hidden, down_flat.T, preferred_element_type=f32).astype(bf16)
    back = back.reshape(2, 2, 2, 2, 2, 2, 2, 4, 2, 2, 2, channels)
    back = back.transpose(0, 3, 1, 4, 6, 2, 8, 5, 9, 7, 10, 11).reshape(kids_dev, PX * PY * PZ, channels)
    child_grad = back[inverse]

    raw_grads = jnp.concatenate(
        [
            raw_down.reshape(8, channels, channels),
            raw_first.reshape(27, channels, channels),
            raw_second.reshape(27, channels, channels),
        ],
        0,
    )
    limit = jnp.float32(channels * math.sqrt(62.0))
    total_values = raw_grads.size
    rows = 8064
    flat = jnp.pad(raw_grads.reshape(-1), (0, rows * channels - total_values)).reshape(rows, channels)
    summed = torus_psum(flat).reshape(-1)[:total_values].reshape(raw_grads.shape)
    grad_total = jnp.sqrt(jnp.sum(summed * summed))
    clipped = summed * jnp.minimum(jnp.float32(1.0), limit / grad_total)
    section_out = from_grid(section.reshape(2 * PX, 2 * PY, PZ, channels))[slot_of]
    return (section_out, child_grad, clipped[:8], clipped[8:35], clipped[35:62])


def solution(mesh):
    in_specs = (
        P("range", None, None),
        P("range", None, None),
        P("range", None),
        P("range", None),
        P(),
        P(),
        P(),
    )
    out_specs = (P("range", None, None), P("range", None, None), P(), P(), P())
    return jax.shard_map(
        on_device, mesh=mesh, in_specs=in_specs, out_specs=out_specs, check_vma=False
    )
```

```python
import math

import jax
import jax.numpy as jnp
from jax import lax
from jax.sharding import PartitionSpec as P

PX = 4
PY = 4
PZ = 8


def to_grid(slots):
    channels = slots.shape[-1]
    g = slots.reshape(2, 2, PX, PY, PZ, channels).transpose(0, 2, 1, 3, 4, 5)
    return g.reshape(2 * PX, 2 * PY, PZ, channels)


def from_grid(grid):
    channels = grid.shape[-1]
    g = grid.reshape(2, PX, 2, PY, PZ, channels).transpose(0, 2, 1, 3, 4, 5)
    return g.reshape(4, PX * PY * PZ, channels)


def padded(grid):
    count = lax.axis_size("range")
    forward = [(i, i + 1) for i in range(count - 1)]
    backward = [(i + 1, i) for i in range(count - 1)]
    low = lax.ppermute(grid[:, :, PZ - 1 :], "range", forward)
    high = lax.ppermute(grid[:, :, :1], "range", backward)
    wide = jnp.concatenate([low, grid, high], axis=2)
    return jnp.pad(wide, ((1, 1), (1, 1), (0, 0), (0, 0)))


def z_columns(pad):
    return jnp.concatenate([pad[:, :, sz : sz + PZ] for sz in range(3)], axis=-1)


def xy_window(zcols, sx, sy):
    return zcols[sx : sx + 2 * PX, sy : sy + 2 * PY].reshape(-1, zcols.shape[-1])


def conv_apply(zcols, weights):
    channels = weights.shape[-1]
    taps = weights.reshape(3, 3, 3 * channels, channels)
    total = None
    for sx in range(3):
        for sy in range(3):
            term = jnp.dot(xy_window(zcols, sx, sy), taps[sx, sy], preferred_element_type=jnp.float32)
            total = term if total is None else total + term
    return total


def conv_weight_grad(zcols, upstream):
    contract_rows = (((0,), (0,)), ((), ()))
    terms = [
        lax.dot_general(xy_window(zcols, sx, sy), upstream, contract_rows, preferred_element_type=jnp.float32)
        for sx in range(3)
        for sy in range(3)
    ]
    return jnp.concatenate(terms, 0)

AXIS_SHIFT = {"y": 1, "x": 3, "z": 5}
PART_ORDERS = (("y", "x", "z"), ("x", "z", "y"), ("z", "y", "x"))


def coordinate(index, shift):
    return (index >> shift) & 3


def partner(index, shift, stage):
    c = (index >> shift) & 3
    other = c ^ 1 if stage == 0 else 3 - c
    return index + ((other - c) << shift)


def keep_bit(c, stage):
    if stage == 0:
        return ((c == 1) | (c == 2)).astype(jnp.int32)
    return (c >= 2).astype(jnp.int32)


def exchange_steps(order):
    return [(AXIS_SHIFT[axis], stage) for axis in order for stage in (0, 1)]


def split_halves(y, bit):
    h = y.shape[0] // 2
    keep = lax.dynamic_slice_in_dim(y, bit * h, h, 0)
    send = lax.dynamic_slice_in_dim(y, (1 - bit) * h, h, 0)
    return keep, send


def join_halves(y, got, bit):
    h = y.shape[0]
    full = jnp.zeros((2 * h,) + y.shape[1:], y.dtype)
    full = lax.dynamic_update_slice_in_dim(full, y, bit * h, 0)
    return lax.dynamic_update_slice_in_dim(full, got, (1 - bit) * h, 0)


def torus_psum(flat):
    count = lax.axis_size("range")
    index = lax.axis_index("range")
    core_perm = [(i, i ^ 1) for i in range(count)]
    core_bit = index & 1
    keep, send = split_halves(flat, core_bit)
    y = keep + lax.ppermute(send, "range", core_perm)
    parts = jnp.split(y, len(PART_ORDERS), 0)
    reduced = []
    for part, order in zip(parts, PART_ORDERS):
        for shift, stage in exchange_steps(order):
            perm = [(i, partner(i, shift, stage)) for i in range(count)]
            bit = keep_bit(coordinate(index, shift), stage)
            keep, send = split_halves(part, bit)
            part = keep + lax.ppermute(send, "range", perm)
        reduced.append(part)
    gathered = []
    for part, order in zip(reduced, PART_ORDERS):
        part = part.astype(jnp.bfloat16)
        for shift, stage in reversed(exchange_steps(order)):
            perm = [(i, partner(i, shift, stage)) for i in range(count)]
            bit = keep_bit(coordinate(index, shift), stage)
            part = join_halves(part, lax.ppermute(part, "range", perm), bit)
        gathered.append(part)
    y = jnp.concatenate(gathered, 0)
    return join_halves(y, lax.ppermute(y, "range", core_perm), core_bit).astype(jnp.float32)


def reversed_kernel(weights):
    return jnp.flip(weights, 0).transpose(0, 2, 1)


def on_device(child_in, cotangent, child_of, neighbours, down_w, first_w, second_w):
    channels = child_in.shape[-1]
    kids_dev = child_in.shape[0]
    own_rank = lax.axis_index("range")
    f32 = jnp.float32
    bf16 = jnp.bfloat16

    slot_of = 2 * (neighbours[:, 4] >= 0).astype(jnp.int32) + (neighbours[:, 10] >= 0).astype(jnp.int32)
    match = slot_of[None, :] == jnp.arange(4, dtype=jnp.int32)[:, None]
    block_at = jnp.sum(jnp.where(match, jnp.arange(4, dtype=jnp.int32)[None, :], 0), axis=1)
    child_rows = child_of - own_rank * kids_dev
    fine_idx = child_rows[block_at].reshape(-1)
    inverse = jnp.zeros((kids_dev,), jnp.int32).at[fine_idx].set(jnp.arange(kids_dev, dtype=jnp.int32))

    fine = child_in[fine_idx].reshape(2, 2, 2, 2, 2, 2, 2, 2, 2, 4, 2, channels)
    patches = fine.transpose(0, 2, 5, 1, 3, 7, 4, 9, 6, 8, 10, 11).reshape(512, 8 * channels)
    down_flat = down_w.reshape(8 * channels, channels)
    hidden = jnp.dot(patches, down_flat, preferred_element_type=f32).astype(bf16)
    hidden_grid = hidden.reshape(2 * PX, 2 * PY, PZ, channels)

    hidden_cols = z_columns(padded(hidden_grid))
    pre_act = conv_apply(hidden_cols, first_w)
    activated = jax.nn.silu(pre_act).astype(bf16)
    act_cols = z_columns(padded(activated.reshape(2 * PX, 2 * PY, PZ, channels)))
    section = (
        hidden.astype(f32) + conv_apply(act_cols, second_w)
    ).astype(bf16)

    cot_grid = to_grid(cotangent[block_at])
    cot_rows = cot_grid.reshape(-1, channels)
    cot_cols = z_columns(padded(cot_grid))
    back_act = conv_apply(cot_cols, reversed_kernel(second_w))
    sigmoid_pre = jax.nn.sigmoid(pre_act)
    d_pre = (back_act * sigmoid_pre * (1.0 + pre_act * (1.0 - sigmoid_pre))).astype(bf16)
    d_pre_cols = z_columns(padded(d_pre.reshape(2 * PX, 2 * PY, PZ, channels)))
    d_hidden = (
        cot_rows.astype(f32)
        + conv_apply(d_pre_cols, reversed_kernel(first_w))
    ).astype(bf16)

    contract_rows = (((0,), (0,)), ((), ()))
    raw_first = conv_weight_grad(hidden_cols, d_pre)
    raw_second = conv_weight_grad(act_cols, cot_rows)
    raw_down = lax.dot_general(patches, d_hidden, contract_rows, preferred_element_type=f32)

    back = jnp.dot(d_hidden, down_flat.T, preferred_element_type=f32).astype(bf16)
    back = back.reshape(2, 2, 2, 2, 2, 2, 2, 4, 2, 2, 2, channels)
    back = back.transpose(0, 3, 1, 4, 6, 2, 8, 5, 9, 7, 10, 11).reshape(kids_dev, PX * PY * PZ, channels)
    child_grad = back[inverse]

    raw_grads = jnp.concatenate(
        [
            raw_down.reshape(8, channels, channels),
            raw_first.reshape(27, channels, channels),
            raw_second.reshape(27, channels, channels),
        ],
        0,
    )
    limit = jnp.float32(channels * math.sqrt(62.0))
    total_values = raw_grads.size
    rows = 8064
    flat = jnp.pad(raw_grads.reshape(-1), (0, rows * channels - total_values)).reshape(rows, channels)
    summed = torus_psum(flat).reshape(-1)[:total_values].reshape(raw_grads.shape)
    grad_total = jnp.sqrt(jnp.sum(summed * summed))
    clipped = summed * jnp.minimum(jnp.float32(1.0), limit / grad_total)
    section_out = from_grid(section.reshape(2 * PX, 2 * PY, PZ, channels))[slot_of]
    return (section_out, child_grad, clipped[:8], clipped[8:35], clipped[35:62])


def solution(mesh):
    in_specs = (
        P("range", None, None),
        P("range", None, None),
        P("range", None),
        P("range", None),
        P(),
        P(),
        P(),
    )
    out_specs = (P("range", None, None), P("range", None, None), P(), P(), P())
    return jax.shard_map(
        on_device, mesh=mesh, in_specs=in_specs, out_specs=out_specs, check_vma=False
    )
```

```python
import math

import jax
import jax.numpy as jnp
from jax import lax
from jax.sharding import PartitionSpec as P

PX = 4
PY = 4
PZ = 8


def to_grid(slots):
    channels = slots.shape[-1]
    g = slots.reshape(2, 2, PX, PY, PZ, channels).transpose(0, 2, 1, 3, 4, 5)
    return g.reshape(2 * PX, 2 * PY, PZ, channels)


def from_grid(grid):
    channels = grid.shape[-1]
    g = grid.reshape(2, PX, 2, PY, PZ, channels).transpose(0, 2, 1, 3, 4, 5)
    return g.reshape(4, PX * PY * PZ, channels)


def padded_many(*grids):
    count = lax.axis_size("range")
    forward = [(i, i + 1) for i in range(count - 1)]
    backward = [(i + 1, i) for i in range(count - 1)]
    low = lax.ppermute(jnp.concatenate([g[:, :, PZ - 1 :] for g in grids], -1), "range", forward)
    high = lax.ppermute(jnp.concatenate([g[:, :, :1] for g in grids], -1), "range", backward)
    out = []
    for n, grid in enumerate(grids):
        width = grid.shape[-1]
        piece = slice(n * width, (n + 1) * width)
        wide = jnp.concatenate([low[..., piece], grid, high[..., piece]], axis=2)
        out.append(jnp.pad(wide, ((1, 1), (1, 1), (0, 0), (0, 0))))
    return out


def padded(grid):
    return padded_many(grid)[0]


def z_columns(pad):
    return jnp.concatenate([pad[:, :, sz : sz + PZ] for sz in range(3)], axis=-1)


def xy_window(zcols, sx, sy):
    return zcols[sx : sx + 2 * PX, sy : sy + 2 * PY].reshape(-1, zcols.shape[-1])


def conv_apply(zcols, weights):
    channels = weights.shape[-1]
    taps = weights.reshape(3, 3, 3 * channels, channels)
    total = None
    for sx in range(3):
        for sy in range(3):
            term = jnp.dot(xy_window(zcols, sx, sy), taps[sx, sy], preferred_element_type=jnp.float32)
            total = term if total is None else total + term
    return total


def conv_weight_grad(zcols, upstream):
    contract_rows = (((0,), (0,)), ((), ()))
    terms = [
        lax.dot_general(xy_window(zcols, sx, sy), upstream, contract_rows, preferred_element_type=jnp.float32)
        for sx in range(3)
        for sy in range(3)
    ]
    return jnp.concatenate(terms, 0)

AXIS_SHIFT = {"y": 1, "x": 3, "z": 5}
PART_ORDERS = (("y", "x", "z"),)


def coordinate(index, shift):
    return (index >> shift) & 3


def partner(index, shift, stage):
    c = (index >> shift) & 3
    other = c ^ 1 if stage == 0 else 3 - c
    return index + ((other - c) << shift)


def keep_bit(c, stage):
    if stage == 0:
        return ((c == 1) | (c == 2)).astype(jnp.int32)
    return (c >= 2).astype(jnp.int32)


def exchange_steps(order):
    return [(AXIS_SHIFT[axis], stage) for axis in order for stage in (0, 1)]


def split_halves(y, bit):
    h = y.shape[0] // 2
    keep = lax.dynamic_slice_in_dim(y, bit * h, h, 0)
    send = lax.dynamic_slice_in_dim(y, (1 - bit) * h, h, 0)
    return keep, send


def join_halves(y, got, bit):
    h = y.shape[0]
    full = jnp.zeros((2 * h,) + y.shape[1:], y.dtype)
    full = lax.dynamic_update_slice_in_dim(full, y, bit * h, 0)
    return lax.dynamic_update_slice_in_dim(full, got, (1 - bit) * h, 0)


def torus_psum(flat):
    count = lax.axis_size("range")
    index = lax.axis_index("range")
    core_perm = [(i, i ^ 1) for i in range(count)]
    core_bit = index & 1
    keep, send = split_halves(flat, core_bit)
    y = keep + lax.ppermute(send, "range", core_perm)
    parts = jnp.split(y, len(PART_ORDERS), 0)
    reduced = []
    for part, order in zip(parts, PART_ORDERS):
        for shift, stage in exchange_steps(order):
            perm = [(i, partner(i, shift, stage)) for i in range(count)]
            bit = keep_bit(coordinate(index, shift), stage)
            keep, send = split_halves(part, bit)
            part = keep + lax.ppermute(send, "range", perm)
        reduced.append(part)
    gathered = []
    for part, order in zip(reduced, PART_ORDERS):
        part = part.astype(jnp.bfloat16)
        for shift, stage in reversed(exchange_steps(order)):
            perm = [(i, partner(i, shift, stage)) for i in range(count)]
            bit = keep_bit(coordinate(index, shift), stage)
            part = join_halves(part, lax.ppermute(part, "range", perm), bit)
        gathered.append(part)
    y = jnp.concatenate(gathered, 0)
    return join_halves(y, lax.ppermute(y, "range", core_perm), core_bit).astype(jnp.float32)


def reversed_kernel(weights):
    return jnp.flip(weights, 0).transpose(0, 2, 1)


def on_device(child_in, cotangent, child_of, neighbours, down_w, first_w, second_w):
    channels = child_in.shape[-1]
    kids_dev = child_in.shape[0]
    own_rank = lax.axis_index("range")
    f32 = jnp.float32
    bf16 = jnp.bfloat16

    slot_of = 2 * (neighbours[:, 4] >= 0).astype(jnp.int32) + (neighbours[:, 10] >= 0).astype(jnp.int32)
    match = slot_of[None, :] == jnp.arange(4, dtype=jnp.int32)[:, None]
    block_at = jnp.sum(jnp.where(match, jnp.arange(4, dtype=jnp.int32)[None, :], 0), axis=1)
    child_rows = child_of - own_rank * kids_dev
    fine_idx = child_rows[block_at].reshape(-1)
    inverse = jnp.zeros((kids_dev,), jnp.int32).at[fine_idx].set(jnp.arange(kids_dev, dtype=jnp.int32))

    fine = child_in[fine_idx].reshape(2, 2, 2, 2, 2, 2, 2, 2, 2, 4, 2, channels)
    patches = fine.transpose(0, 2, 5, 1, 3, 7, 4, 9, 6, 8, 10, 11).reshape(512, 8 * channels)
    down_flat = down_w.reshape(8 * channels, channels)
    hidden = jnp.dot(patches, down_flat, preferred_element_type=f32).astype(bf16)
    hidden_grid = hidden.reshape(2 * PX, 2 * PY, PZ, channels)

    cot_grid = to_grid(cotangent[block_at])
    hidden_pad, cot_pad = padded_many(hidden_grid, cot_grid)
    hidden_cols = z_columns(hidden_pad)
    pre_act = conv_apply(hidden_cols, first_w)
    activated = jax.nn.silu(pre_act).astype(bf16)
    act_cols = z_columns(padded(activated.reshape(2 * PX, 2 * PY, PZ, channels)))
    section = (
        hidden.astype(f32) + conv_apply(act_cols, second_w)
    ).astype(bf16)

    cot_rows = cot_grid.reshape(-1, channels)
    cot_cols = z_columns(cot_pad)
    back_act = conv_apply(cot_cols, reversed_kernel(second_w))
    sigmoid_pre = jax.nn.sigmoid(pre_act)
    d_pre = (back_act * sigmoid_pre * (1.0 + pre_act * (1.0 - sigmoid_pre))).astype(bf16)
    d_pre_cols = z_columns(padded(d_pre.reshape(2 * PX, 2 * PY, PZ, channels)))
    d_hidden = (
        cot_rows.astype(f32)
        + conv_apply(d_pre_cols, reversed_kernel(first_w))
    ).astype(bf16)

    contract_rows = (((0,), (0,)), ((), ()))
    raw_first = conv_weight_grad(hidden_cols, d_pre)
    raw_second = conv_weight_grad(act_cols, cot_rows)
    raw_down = lax.dot_general(patches, d_hidden, contract_rows, preferred_element_type=f32)

    back = jnp.dot(d_hidden, down_flat.T, preferred_element_type=f32).astype(bf16)
    back = back.reshape(2, 2, 2, 2, 2, 2, 2, 4, 2, 2, 2, channels)
    back = back.transpose(0, 3, 1, 4, 6, 2, 8, 5, 9, 7, 10, 11).reshape(kids_dev, PX * PY * PZ, channels)
    child_grad = back[inverse]

    raw_grads = jnp.concatenate(
        [
            raw_down.reshape(8, channels, channels),
            raw_first.reshape(27, channels, channels),
            raw_second.reshape(27, channels, channels),
        ],
        0,
    )
    limit = jnp.float32(channels * math.sqrt(62.0))
    total_values = raw_grads.size
    rows = total_values // channels
    flat = jnp.pad(raw_grads.reshape(-1), (0, rows * channels - total_values)).reshape(rows, channels)
    summed = torus_psum(flat).reshape(-1)[:total_values].reshape(raw_grads.shape)
    grad_total = jnp.sqrt(jnp.sum(summed * summed))
    clipped = summed * jnp.minimum(jnp.float32(1.0), limit / grad_total)
    section_out = from_grid(section.reshape(2 * PX, 2 * PY, PZ, channels))[slot_of]
    return (section_out, child_grad, clipped[:8], clipped[8:35], clipped[35:62])


def solution(mesh):
    in_specs = (
        P("range", None, None),
        P("range", None, None),
        P("range", None),
        P("range", None),
        P(),
        P(),
        P(),
    )
    out_specs = (P("range", None, None), P("range", None, None), P(), P(), P())
    return jax.shard_map(
        on_device, mesh=mesh, in_specs=in_specs, out_specs=out_specs, check_vma=False
    )
```

```python
import math

import jax
import jax.numpy as jnp
from jax import lax
from jax.sharding import PartitionSpec as P

PX = 4
PY = 4
PZ = 8


def to_grid(slots):
    channels = slots.shape[-1]
    g = slots.reshape(2, 2, PX, PY, PZ, channels).transpose(0, 2, 1, 3, 4, 5)
    return g.reshape(2 * PX, 2 * PY, PZ, channels)


def from_grid(grid):
    channels = grid.shape[-1]
    g = grid.reshape(2, PX, 2, PY, PZ, channels).transpose(0, 2, 1, 3, 4, 5)
    return g.reshape(4, PX * PY * PZ, channels)


def padded_many(*grids):
    count = lax.axis_size("range")
    forward = [(i, i + 1) for i in range(count - 1)]
    backward = [(i + 1, i) for i in range(count - 1)]
    low = lax.ppermute(jnp.concatenate([g[:, :, PZ - 1 :] for g in grids], -1), "range", forward)
    high = lax.ppermute(jnp.concatenate([g[:, :, :1] for g in grids], -1), "range", backward)
    out = []
    for n, grid in enumerate(grids):
        width = grid.shape[-1]
        piece = slice(n * width, (n + 1) * width)
        wide = jnp.concatenate([low[..., piece], grid, high[..., piece]], axis=2)
        out.append(jnp.pad(wide, ((1, 1), (1, 1), (0, 0), (0, 0))))
    return out


def padded(grid):
    return padded_many(grid)[0]


def z_columns(pad):
    return jnp.concatenate([pad[:, :, sz : sz + PZ] for sz in range(3)], axis=-1)


def xy_window(zcols, sx, sy):
    return zcols[sx : sx + 2 * PX, sy : sy + 2 * PY].reshape(-1, zcols.shape[-1])


def conv_apply(zcols, weights):
    channels = weights.shape[-1]
    taps = weights.reshape(3, 3, 3 * channels, channels)
    total = None
    for sx in range(3):
        for sy in range(3):
            term = jnp.dot(xy_window(zcols, sx, sy), taps[sx, sy], preferred_element_type=jnp.float32)
            total = term if total is None else total + term
    return total


def conv_weight_grad(zcols, upstream):
    contract_rows = (((0,), (0,)), ((), ()))
    terms = [
        lax.dot_general(xy_window(zcols, sx, sy), upstream, contract_rows, preferred_element_type=jnp.float32)
        for sx in range(3)
        for sy in range(3)
    ]
    return jnp.concatenate(terms, 0)

AXIS_SHIFT = {"y": 1, "x": 3, "z": 5}
PART_ORDERS = (("y", "x", "z"), ("x", "z", "y"), ("z", "y", "x"))


def coordinate(index, shift):
    return (index >> shift) & 3


def partner(index, shift, stage):
    c = (index >> shift) & 3
    other = c ^ 1 if stage == 0 else 3 - c
    return index + ((other - c) << shift)


def keep_bit(c, stage):
    if stage == 0:
        return ((c == 1) | (c == 2)).astype(jnp.int32)
    return (c >= 2).astype(jnp.int32)


def exchange_steps(order):
    return [(AXIS_SHIFT[axis], stage) for axis in order for stage in (0, 1)]


def split_halves(y, bit):
    h = y.shape[0] // 2
    keep = lax.dynamic_slice_in_dim(y, bit * h, h, 0)
    send = lax.dynamic_slice_in_dim(y, (1 - bit) * h, h, 0)
    return keep, send


def join_halves(y, got, bit):
    h = y.shape[0]
    full = jnp.zeros((2 * h,) + y.shape[1:], y.dtype)
    full = lax.dynamic_update_slice_in_dim(full, y, bit * h, 0)
    return lax.dynamic_update_slice_in_dim(full, got, (1 - bit) * h, 0)


def torus_psum(flat):
    count = lax.axis_size("range")
    index = lax.axis_index("range")
    core_perm = [(i, i ^ 1) for i in range(count)]
    core_bit = index & 1
    keep, send = split_halves(flat, core_bit)
    y = keep + lax.ppermute(send, "range", core_perm)
    parts = jnp.split(y, len(PART_ORDERS), 0)
    reduced = []
    for part, order in zip(parts, PART_ORDERS):
        for shift, stage in exchange_steps(order[:1]):
            perm = [(i, partner(i, shift, stage)) for i in range(count)]
            bit = keep_bit(coordinate(index, shift), stage)
            keep, send = split_halves(part, bit)
            part = keep + lax.ppermute(send, "range", perm)
        for shift, stage in exchange_steps(order[1:]):
            perm = [(i, partner(i, shift, stage)) for i in range(count)]
            part = part + lax.ppermute(part, "range", perm)
        reduced.append(part)
    gathered = []
    for part, order in zip(reduced, PART_ORDERS):
        part = part.astype(jnp.bfloat16)
        for shift, stage in reversed(exchange_steps(order[:1])):
            perm = [(i, partner(i, shift, stage)) for i in range(count)]
            bit = keep_bit(coordinate(index, shift), stage)
            part = join_halves(part, lax.ppermute(part, "range", perm), bit)
        gathered.append(part)
    y = jnp.concatenate(gathered, 0)
    return join_halves(y, lax.ppermute(y, "range", core_perm), core_bit).astype(jnp.float32)


def reversed_kernel(weights):
    return jnp.flip(weights, 0).transpose(0, 2, 1)


def on_device(child_in, cotangent, child_of, neighbours, down_w, first_w, second_w):
    channels = child_in.shape[-1]
    kids_dev = child_in.shape[0]
    own_rank = lax.axis_index("range")
    f32 = jnp.float32
    bf16 = jnp.bfloat16

    slot_of = 2 * (neighbours[:, 4] >= 0).astype(jnp.int32) + (neighbours[:, 10] >= 0).astype(jnp.int32)
    match = slot_of[None, :] == jnp.arange(4, dtype=jnp.int32)[:, None]
    block_at = jnp.sum(jnp.where(match, jnp.arange(4, dtype=jnp.int32)[None, :], 0), axis=1)
    child_rows = child_of - own_rank * kids_dev
    fine_idx = child_rows[block_at].reshape(-1)
    inverse = jnp.zeros((kids_dev,), jnp.int32).at[fine_idx].set(jnp.arange(kids_dev, dtype=jnp.int32))

    fine = child_in[fine_idx].reshape(2, 2, 2, 2, 2, 2, 2, 2, 2, 4, 2, channels)
    patches = fine.transpose(0, 2, 5, 1, 3, 7, 4, 9, 6, 8, 10, 11).reshape(512, 8 * channels)
    down_flat = down_w.reshape(8 * channels, channels)
    hidden = jnp.dot(patches, down_flat, preferred_element_type=f32).astype(bf16)
    hidden_grid = hidden.reshape(2 * PX, 2 * PY, PZ, channels)

    cot_grid = to_grid(cotangent[block_at])
    hidden_pad, cot_pad = padded_many(hidden_grid, cot_grid)
    hidden_cols = z_columns(hidden_pad)
    pre_act = conv_apply(hidden_cols, first_w)
    activated = jax.nn.silu(pre_act).astype(bf16)
    act_cols = z_columns(padded(activated.reshape(2 * PX, 2 * PY, PZ, channels)))
    section = (
        hidden.astype(f32) + conv_apply(act_cols, second_w)
    ).astype(bf16)

    cot_rows = cot_grid.reshape(-1, channels)
    cot_cols = z_columns(cot_pad)
    back_act = conv_apply(cot_cols, reversed_kernel(second_w))
    sigmoid_pre = jax.nn.sigmoid(pre_act)
    d_pre = (back_act * sigmoid_pre * (1.0 + pre_act * (1.0 - sigmoid_pre))).astype(bf16)
    d_pre_cols = z_columns(padded(d_pre.reshape(2 * PX, 2 * PY, PZ, channels)))
    d_hidden = (
        cot_rows.astype(f32)
        + conv_apply(d_pre_cols, reversed_kernel(first_w))
    ).astype(bf16)

    contract_rows = (((0,), (0,)), ((), ()))
    raw_first = conv_weight_grad(hidden_cols, d_pre)
    raw_second = conv_weight_grad(act_cols, cot_rows)
    raw_down = lax.dot_general(patches, d_hidden, contract_rows, preferred_element_type=f32)

    back = jnp.dot(d_hidden, down_flat.T, preferred_element_type=f32).astype(bf16)
    back = back.reshape(2, 2, 2, 2, 2, 2, 2, 4, 2, 2, 2, channels)
    back = back.transpose(0, 3, 1, 4, 6, 2, 8, 5, 9, 7, 10, 11).reshape(kids_dev, PX * PY * PZ, channels)
    child_grad = back[inverse]

    raw_grads = jnp.concatenate(
        [
            raw_down.reshape(8, channels, channels),
            raw_first.reshape(27, channels, channels),
            raw_second.reshape(27, channels, channels),
        ],
        0,
    )
    limit = jnp.float32(channels * math.sqrt(62.0))
    total_values = raw_grads.size
    rows = 8064
    flat = jnp.pad(raw_grads.reshape(-1), (0, rows * channels - total_values)).reshape(rows, channels)
    summed = torus_psum(flat).reshape(-1)[:total_values].reshape(raw_grads.shape)
    grad_total = jnp.sqrt(jnp.sum(summed * summed))
    clipped = summed * jnp.minimum(jnp.float32(1.0), limit / grad_total)
    section_out = from_grid(section.reshape(2 * PX, 2 * PY, PZ, channels))[slot_of]
    return (section_out, child_grad, clipped[:8], clipped[8:35], clipped[35:62])


def solution(mesh):
    in_specs = (
        P("range", None, None),
        P("range", None, None),
        P("range", None),
        P("range", None),
        P(),
        P(),
        P(),
    )
    out_specs = (P("range", None, None), P("range", None, None), P(), P(), P())
    return jax.shard_map(
        on_device, mesh=mesh, in_specs=in_specs, out_specs=out_specs, check_vma=False
    )
```

```python
import math

import jax
import jax.numpy as jnp
from jax import lax
from jax.sharding import PartitionSpec as P

PX = 4
PY = 4
PZ = 8


def to_grid(slots):
    channels = slots.shape[-1]
    g = slots.reshape(2, 2, PX, PY, PZ, channels).transpose(0, 2, 1, 3, 4, 5)
    return g.reshape(2 * PX, 2 * PY, PZ, channels)


def from_grid(grid):
    channels = grid.shape[-1]
    g = grid.reshape(2, PX, 2, PY, PZ, channels).transpose(0, 2, 1, 3, 4, 5)
    return g.reshape(4, PX * PY * PZ, channels)


def padded_many(*grids):
    count = lax.axis_size("range")
    forward = [(i, i + 1) for i in range(count - 1)]
    backward = [(i + 1, i) for i in range(count - 1)]
    low = lax.ppermute(jnp.concatenate([g[:, :, PZ - 1 :] for g in grids], -1), "range", forward)
    high = lax.ppermute(jnp.concatenate([g[:, :, :1] for g in grids], -1), "range", backward)
    out = []
    for n, grid in enumerate(grids):
        width = grid.shape[-1]
        piece = slice(n * width, (n + 1) * width)
        wide = jnp.concatenate([low[..., piece], grid, high[..., piece]], axis=2)
        out.append(jnp.pad(wide, ((1, 1), (1, 1), (0, 0), (0, 0))))
    return out


def padded(grid):
    return padded_many(grid)[0]


def widened(depth, *grids):
    count = lax.axis_size("range")
    forward = [(i, i + 1) for i in range(count - 1)]
    backward = [(i + 1, i) for i in range(count - 1)]
    low = lax.ppermute(jnp.concatenate([g[:, :, PZ - depth :] for g in grids], -1), "range", forward)
    high = lax.ppermute(jnp.concatenate([g[:, :, :depth] for g in grids], -1), "range", backward)
    out = []
    for n, grid in enumerate(grids):
        width = grid.shape[-1]
        piece = slice(n * width, (n + 1) * width)
        out.append(jnp.concatenate([low[..., piece], grid, high[..., piece]], axis=2))
    return out


def xy_padded(grid):
    return jnp.pad(grid, ((1, 1), (1, 1), (0, 0), (0, 0)))


def z_columns_n(pad, planes):
    return jnp.concatenate([pad[:, :, sz : sz + planes] for sz in range(3)], axis=-1)


def z_columns(pad):
    return jnp.concatenate([pad[:, :, sz : sz + PZ] for sz in range(3)], axis=-1)


def xy_window(zcols, sx, sy):
    return zcols[sx : sx + 2 * PX, sy : sy + 2 * PY].reshape(-1, zcols.shape[-1])


def conv_apply(zcols, weights):
    channels = weights.shape[-1]
    taps = weights.reshape(3, 3, 3 * channels, channels)
    total = None
    for sx in range(3):
        for sy in range(3):
            term = jnp.dot(xy_window(zcols, sx, sy), taps[sx, sy], preferred_element_type=jnp.float32)
            total = term if total is None else total + term
    return total


def conv_weight_grad(zcols, upstream):
    contract_rows = (((0,), (0,)), ((), ()))
    terms = [
        lax.dot_general(xy_window(zcols, sx, sy), upstream, contract_rows, preferred_element_type=jnp.float32)
        for sx in range(3)
        for sy in range(3)
    ]
    return jnp.concatenate(terms, 0)

AXIS_SHIFT = {"y": 1, "x": 3, "z": 5}
PART_ORDERS = (("y", "x", "z"), ("x", "z", "y"), ("z", "y", "x"))


def coordinate(index, shift):
    return (index >> shift) & 3


def partner(index, shift, stage):
    c = (index >> shift) & 3
    other = c ^ 1 if stage == 0 else 3 - c
    return index + ((other - c) << shift)


def keep_bit(c, stage):
    if stage == 0:
        return ((c == 1) | (c == 2)).astype(jnp.int32)
    return (c >= 2).astype(jnp.int32)


def exchange_steps(order):
    return [(AXIS_SHIFT[axis], stage) for axis in order for stage in (0, 1)]


def split_halves(y, bit):
    h = y.shape[0] // 2
    keep = lax.dynamic_slice_in_dim(y, bit * h, h, 0)
    send = lax.dynamic_slice_in_dim(y, (1 - bit) * h, h, 0)
    return keep, send


def join_halves(y, got, bit):
    h = y.shape[0]
    full = jnp.zeros((2 * h,) + y.shape[1:], y.dtype)
    full = lax.dynamic_update_slice_in_dim(full, y, bit * h, 0)
    return lax.dynamic_update_slice_in_dim(full, got, (1 - bit) * h, 0)


def torus_psum(flat):
    count = lax.axis_size("range")
    index = lax.axis_index("range")
    core_perm = [(i, i ^ 1) for i in range(count)]
    core_bit = index & 1
    keep, send = split_halves(flat, core_bit)
    y = keep + lax.ppermute(send, "range", core_perm)
    parts = jnp.split(y, len(PART_ORDERS), 0)
    reduced = []
    for part, order in zip(parts, PART_ORDERS):
        for shift, stage in exchange_steps(order[:1]):
            perm = [(i, partner(i, shift, stage)) for i in range(count)]
            bit = keep_bit(coordinate(index, shift), stage)
            keep, send = split_halves(part, bit)
            part = keep + lax.ppermute(send, "range", perm)
        for shift, stage in exchange_steps(order[1:]):
            perm = [(i, partner(i, shift, stage)) for i in range(count)]
            part = part + lax.ppermute(part, "range", perm)
        reduced.append(part)
    gathered = []
    for part, order in zip(reduced, PART_ORDERS):
        part = part.astype(jnp.bfloat16)
        for shift, stage in reversed(exchange_steps(order[:1])):
            perm = [(i, partner(i, shift, stage)) for i in range(count)]
            bit = keep_bit(coordinate(index, shift), stage)
            part = join_halves(part, lax.ppermute(part, "range", perm), bit)
        gathered.append(part)
    y = jnp.concatenate(gathered, 0)
    return join_halves(y, lax.ppermute(y, "range", core_perm), core_bit).astype(jnp.float32)


def reversed_kernel(weights):
    return jnp.flip(weights, 0).transpose(0, 2, 1)


def on_device(child_in, cotangent, child_of, neighbours, down_w, first_w, second_w):
    channels = child_in.shape[-1]
    kids_dev = child_in.shape[0]
    own_rank = lax.axis_index("range")
    f32 = jnp.float32
    bf16 = jnp.bfloat16

    slot_of = 2 * (neighbours[:, 4] >= 0).astype(jnp.int32) + (neighbours[:, 10] >= 0).astype(jnp.int32)
    match = slot_of[None, :] == jnp.arange(4, dtype=jnp.int32)[:, None]
    block_at = jnp.sum(jnp.where(match, jnp.arange(4, dtype=jnp.int32)[None, :], 0), axis=1)
    child_rows = child_of - own_rank * kids_dev
    fine_idx = child_rows[block_at].reshape(-1)
    inverse = jnp.zeros((kids_dev,), jnp.int32).at[fine_idx].set(jnp.arange(kids_dev, dtype=jnp.int32))

    fine = child_in[fine_idx].reshape(2, 2, 2, 2, 2, 2, 2, 2, 2, 4, 2, channels)
    patches = fine.transpose(0, 2, 5, 1, 3, 7, 4, 9, 6, 8, 10, 11).reshape(512, 8 * channels)
    down_flat = down_w.reshape(8 * channels, channels)
    hidden = jnp.dot(patches, down_flat, preferred_element_type=f32).astype(bf16)
    hidden_grid = hidden.reshape(2 * PX, 2 * PY, PZ, channels)

    cot_grid = to_grid(cotangent[block_at])
    cot_rows = cot_grid.reshape(-1, channels)
    hidden_wide, cot_wide = widened(2, hidden_grid, cot_grid)
    hidden_pad = xy_padded(hidden_wide)
    cot_pad = xy_padded(cot_wide)
    count = lax.axis_size("range")
    planes = PZ + 2
    plane = jnp.arange(planes, dtype=jnp.int32)
    plane_ok = ((plane > 0) | (own_rank > 0)) & ((plane < planes - 1) | (own_rank < count - 1))
    plane_ok = plane_ok.reshape(1, 1, planes, 1)
    pre_wide = conv_apply(z_columns_n(hidden_pad, planes), first_w).reshape(2 * PX, 2 * PY, planes, channels)
    act_wide = jnp.where(plane_ok, jax.nn.silu(pre_wide), 0.0).astype(bf16)
    act_cols = z_columns(xy_padded(act_wide))
    section = (
        hidden.astype(f32) + conv_apply(act_cols, second_w)
    ).astype(bf16)

    back_wide = conv_apply(z_columns_n(cot_pad, planes), reversed_kernel(second_w)).reshape(pre_wide.shape)
    sigmoid_pre = jax.nn.sigmoid(pre_wide)
    d_pre_wide = jnp.where(
        plane_ok, back_wide * sigmoid_pre * (1.0 + pre_wide * (1.0 - sigmoid_pre)), 0.0
    ).astype(bf16)
    d_pre = d_pre_wide[:, :, 1 : PZ + 1].reshape(-1, channels)
    d_pre_cols = z_columns(xy_padded(d_pre_wide))
    d_hidden = (
        cot_rows.astype(f32)
        + conv_apply(d_pre_cols, reversed_kernel(first_w))
    ).astype(bf16)
    hidden_cols = z_columns(hidden_pad[:, :, 1 : PZ + 3])

    contract_rows = (((0,), (0,)), ((), ()))
    raw_first = conv_weight_grad(hidden_cols, d_pre)
    raw_second = conv_weight_grad(act_cols, cot_rows)
    raw_down = lax.dot_general(patches, d_hidden, contract_rows, preferred_element_type=f32)

    back = jnp.dot(d_hidden, down_flat.T, preferred_element_type=f32).astype(bf16)
    back = back.reshape(2, 2, 2, 2, 2, 2, 2, 4, 2, 2, 2, channels)
    back = back.transpose(0, 3, 1, 4, 6, 2, 8, 5, 9, 7, 10, 11).reshape(kids_dev, PX * PY * PZ, channels)
    child_grad = back[inverse]

    raw_grads = jnp.concatenate(
        [
            raw_down.reshape(8, channels, channels),
            raw_first.reshape(27, channels, channels),
            raw_second.reshape(27, channels, channels),
        ],
        0,
    )
    limit = jnp.float32(channels * math.sqrt(62.0))
    total_values = raw_grads.size
    rows = 8064
    flat = jnp.pad(raw_grads.reshape(-1), (0, rows * channels - total_values)).reshape(rows, channels)
    summed = torus_psum(flat).reshape(-1)[:total_values].reshape(raw_grads.shape)
    grad_total = jnp.sqrt(jnp.sum(summed * summed))
    clipped = summed * jnp.minimum(jnp.float32(1.0), limit / grad_total)
    section_out = from_grid(section.reshape(2 * PX, 2 * PY, PZ, channels))[slot_of]
    return (section_out, child_grad, clipped[:8], clipped[8:35], clipped[35:62])


def solution(mesh):
    in_specs = (
        P("range", None, None),
        P("range", None, None),
        P("range", None),
        P("range", None),
        P(),
        P(),
        P(),
    )
    out_specs = (P("range", None, None), P("range", None, None), P(), P(), P())
    return jax.shard_map(
        on_device, mesh=mesh, in_specs=in_specs, out_specs=out_specs, check_vma=False
    )
```

```python
import math

import jax
import jax.numpy as jnp
from jax import lax
from jax.sharding import PartitionSpec as P

PX = 4
PY = 4
PZ = 8


def to_grid(slots):
    channels = slots.shape[-1]
    g = slots.reshape(2, 2, PX, PY, PZ, channels).transpose(0, 2, 1, 3, 4, 5)
    return g.reshape(2 * PX, 2 * PY, PZ, channels)


def from_grid(grid):
    channels = grid.shape[-1]
    g = grid.reshape(2, PX, 2, PY, PZ, channels).transpose(0, 2, 1, 3, 4, 5)
    return g.reshape(4, PX * PY * PZ, channels)


def padded_many(*grids):
    count = lax.axis_size("range")
    forward = [(i, i + 1) for i in range(count - 1)]
    backward = [(i + 1, i) for i in range(count - 1)]
    low = lax.ppermute(jnp.concatenate([g[:, :, PZ - 1 :] for g in grids], -1), "range", forward)
    high = lax.ppermute(jnp.concatenate([g[:, :, :1] for g in grids], -1), "range", backward)
    out = []
    for n, grid in enumerate(grids):
        width = grid.shape[-1]
        piece = slice(n * width, (n + 1) * width)
        wide = jnp.concatenate([low[..., piece], grid, high[..., piece]], axis=2)
        out.append(jnp.pad(wide, ((1, 1), (1, 1), (0, 0), (0, 0))))
    return out


def padded(grid):
    return padded_many(grid)[0]


def widened(depth, *grids):
    count = lax.axis_size("range")
    forward = [(i, i + 1) for i in range(count - 1)]
    backward = [(i + 1, i) for i in range(count - 1)]
    low = lax.ppermute(jnp.concatenate([g[:, :, PZ - depth :] for g in grids], -1), "range", forward)
    high = lax.ppermute(jnp.concatenate([g[:, :, :depth] for g in grids], -1), "range", backward)
    out = []
    for n, grid in enumerate(grids):
        width = grid.shape[-1]
        piece = slice(n * width, (n + 1) * width)
        out.append(jnp.concatenate([low[..., piece], grid, high[..., piece]], axis=2))
    return out


def xy_padded(grid):
    return jnp.pad(grid, ((1, 1), (1, 1), (0, 0), (0, 0)))


def z_columns_n(pad, planes):
    return jnp.concatenate([pad[:, :, sz : sz + planes] for sz in range(3)], axis=-1)


def z_columns(pad):
    return jnp.concatenate([pad[:, :, sz : sz + PZ] for sz in range(3)], axis=-1)


def xy_window(zcols, sx, sy):
    return zcols[sx : sx + 2 * PX, sy : sy + 2 * PY].reshape(-1, zcols.shape[-1])


def conv_apply(zcols, weights):
    channels = weights.shape[-1]
    taps = weights.reshape(3, 3, 3 * channels, channels)
    total = None
    for sx in range(3):
        for sy in range(3):
            term = jnp.dot(xy_window(zcols, sx, sy), taps[sx, sy], preferred_element_type=jnp.float32)
            total = term if total is None else total + term
    return total


def conv_weight_grad(zcols, upstream):
    contract_rows = (((0,), (0,)), ((), ()))
    terms = [
        lax.dot_general(xy_window(zcols, sx, sy), upstream, contract_rows, preferred_element_type=jnp.float32)
        for sx in range(3)
        for sy in range(3)
    ]
    return jnp.concatenate(terms, 0)

AXIS_SHIFT = {"y": 1, "x": 3, "z": 5}
PART_ORDERS = (("y", "x", "z"), ("x", "z", "y"), ("z", "y", "x"))


def coordinate(index, shift):
    return (index >> shift) & 3


def partner(index, shift, stage):
    c = (index >> shift) & 3
    other = c ^ 1 if stage == 0 else 3 - c
    return index + ((other - c) << shift)


def keep_bit(c, stage):
    if stage == 0:
        return ((c == 1) | (c == 2)).astype(jnp.int32)
    return (c >= 2).astype(jnp.int32)


def exchange_steps(order):
    return [(AXIS_SHIFT[axis], stage) for axis in order for stage in (0, 1)]


def split_halves(y, bit):
    h = y.shape[0] // 2
    keep = lax.dynamic_slice_in_dim(y, bit * h, h, 0)
    send = lax.dynamic_slice_in_dim(y, (1 - bit) * h, h, 0)
    return keep, send


def join_halves(y, got, bit):
    h = y.shape[0]
    full = jnp.zeros((2 * h,) + y.shape[1:], y.dtype)
    full = lax.dynamic_update_slice_in_dim(full, y, bit * h, 0)
    return lax.dynamic_update_slice_in_dim(full, got, (1 - bit) * h, 0)


def torus_psum(flat):
    count = lax.axis_size("range")
    index = lax.axis_index("range")
    core_perm = [(i, i ^ 1) for i in range(count)]
    core_bit = index & 1
    keep, send = split_halves(flat, core_bit)
    y = keep + lax.ppermute(send, "range", core_perm)
    parts = jnp.split(y, len(PART_ORDERS), 0)
    reduced = []
    for part, order in zip(parts, PART_ORDERS):
        for shift, stage in exchange_steps(order[:1]):
            perm = [(i, partner(i, shift, stage)) for i in range(count)]
            bit = keep_bit(coordinate(index, shift), stage)
            keep, send = split_halves(part, bit)
            part = keep + lax.ppermute(send, "range", perm)
        for shift, stage in exchange_steps(order[1:]):
            perm = [(i, partner(i, shift, stage)) for i in range(count)]
            part = part + lax.ppermute(part, "range", perm)
        reduced.append(part)
    gathered = []
    for part, order in zip(reduced, PART_ORDERS):
        part = part.astype(jnp.bfloat16)
        for shift, stage in reversed(exchange_steps(order[:1])):
            perm = [(i, partner(i, shift, stage)) for i in range(count)]
            bit = keep_bit(coordinate(index, shift), stage)
            part = join_halves(part, lax.ppermute(part, "range", perm), bit)
        gathered.append(part)
    y = jnp.concatenate(gathered, 0)
    return join_halves(y, lax.ppermute(y, "range", core_perm), core_bit).astype(jnp.float32)


def reversed_kernel(weights):
    return jnp.flip(weights, 0).transpose(0, 2, 1)


def on_device(child_in, cotangent, child_of, neighbours, down_w, first_w, second_w):
    channels = child_in.shape[-1]
    kids_dev = child_in.shape[0]
    own_rank = lax.axis_index("range")
    f32 = jnp.float32
    bf16 = jnp.bfloat16

    slot_of = 2 * (neighbours[:, 4] >= 0).astype(jnp.int32) + (neighbours[:, 10] >= 0).astype(jnp.int32)
    match = slot_of[None, :] == jnp.arange(4, dtype=jnp.int32)[:, None]
    block_at = jnp.sum(jnp.where(match, jnp.arange(4, dtype=jnp.int32)[None, :], 0), axis=1)
    child_rows = child_of - own_rank * kids_dev
    fine_idx = child_rows[block_at].reshape(-1)
    inverse = jnp.zeros((kids_dev,), jnp.int32).at[fine_idx].set(jnp.arange(kids_dev, dtype=jnp.int32))

    fine = child_in[fine_idx].reshape(2, 2, 2, 2, 2, 2, 2, 2, 2, 4, 2, channels)
    patches = fine.transpose(0, 2, 5, 1, 3, 7, 4, 9, 6, 8, 10, 11).reshape(512, 8 * channels)
    down_flat = down_w.reshape(8 * channels, channels)
    hidden = jnp.dot(patches, down_flat, preferred_element_type=f32).astype(bf16)
    hidden_grid = hidden.reshape(2 * PX, 2 * PY, PZ, channels)

    cot_grid = to_grid(cotangent[block_at])
    cot_rows = cot_grid.reshape(-1, channels)
    hidden_wide, cot_wide = widened(2, hidden_grid, cot_grid)
    hidden_pad = xy_padded(hidden_wide)
    cot_pad = xy_padded(cot_wide)
    count = lax.axis_size("range")
    side_ok = jnp.stack([own_rank > 0, own_rank < count - 1]).reshape(2, 1, 1, 1)

    def halo_conv(pad, weights):
        sides = [jnp.concatenate([pad[:, :, t + sz] for sz in range(3)], -1) for t in (0, PZ + 1)]
        zc = jnp.stack(sides, 0)
        channels_out = weights.shape[-1]
        taps = weights.reshape(3, 3, -1, channels_out)
        total = None
        for sx in range(3):
            for sy in range(3):
                win = zc[:, sx : sx + 2 * PX, sy : sy + 2 * PY].reshape(-1, zc.shape[-1])
                term = jnp.dot(win, taps[sx, sy], preferred_element_type=f32)
                total = term if total is None else total + term
        return total.reshape(2, 2 * PX, 2 * PY, channels_out)

    def with_halo(own, halo):
        return jnp.concatenate([halo[0][:, :, None], own, halo[1][:, :, None]], axis=2)

    hidden_cols = z_columns(hidden_pad[:, :, 1 : PZ + 3])
    pre_act = conv_apply(hidden_cols, first_w)
    pre_halo = halo_conv(hidden_pad, first_w)
    act_own = jax.nn.silu(pre_act).astype(bf16).reshape(2 * PX, 2 * PY, PZ, channels)
    act_halo = jnp.where(side_ok, jax.nn.silu(pre_halo), 0.0).astype(bf16)
    act_cols = z_columns(xy_padded(with_halo(act_own, act_halo)))
    section = (
        hidden.astype(f32) + conv_apply(act_cols, second_w)
    ).astype(bf16)

    def d_pre_of(back, pre):
        sig = jax.nn.sigmoid(pre)
        return back * sig * (1.0 + pre * (1.0 - sig))

    cot_cols = z_columns(cot_pad[:, :, 1 : PZ + 3])
    back_act = conv_apply(cot_cols, reversed_kernel(second_w))
    back_halo = halo_conv(cot_pad, reversed_kernel(second_w))
    d_pre = d_pre_of(back_act, pre_act).astype(bf16)
    d_pre_halo = jnp.where(side_ok, d_pre_of(back_halo, pre_halo), 0.0).astype(bf16)
    d_pre_cols = z_columns(xy_padded(with_halo(d_pre.reshape(2 * PX, 2 * PY, PZ, channels), d_pre_halo)))
    d_hidden = (
        cot_rows.astype(f32)
        + conv_apply(d_pre_cols, reversed_kernel(first_w))
    ).astype(bf16)

    contract_rows = (((0,), (0,)), ((), ()))
    raw_first = conv_weight_grad(hidden_cols, d_pre)
    raw_second = conv_weight_grad(act_cols, cot_rows)
    raw_down = lax.dot_general(patches, d_hidden, contract_rows, preferred_element_type=f32)

    back = jnp.dot(d_hidden, down_flat.T, preferred_element_type=f32).astype(bf16)
    back = back.reshape(2, 2, 2, 2, 2, 2, 2, 4, 2, 2, 2, channels)
    back = back.transpose(0, 3, 1, 4, 6, 2, 8, 5, 9, 7, 10, 11).reshape(kids_dev, PX * PY * PZ, channels)
    child_grad = back[inverse]

    raw_grads = jnp.concatenate(
        [
            raw_down.reshape(8, channels, channels),
            raw_first.reshape(27, channels, channels),
            raw_second.reshape(27, channels, channels),
        ],
        0,
    )
    limit = jnp.float32(channels * math.sqrt(62.0))
    total_values = raw_grads.size
    rows = 8064
    flat = jnp.pad(raw_grads.reshape(-1), (0, rows * channels - total_values)).reshape(rows, channels)
    summed = torus_psum(flat).reshape(-1)[:total_values].reshape(raw_grads.shape)
    grad_total = jnp.sqrt(jnp.sum(summed * summed))
    clipped = summed * jnp.minimum(jnp.float32(1.0), limit / grad_total)
    section_out = from_grid(section.reshape(2 * PX, 2 * PY, PZ, channels))[slot_of]
    return (section_out, child_grad, clipped[:8], clipped[8:35], clipped[35:62])


def solution(mesh):
    in_specs = (
        P("range", None, None),
        P("range", None, None),
        P("range", None),
        P("range", None),
        P(),
        P(),
        P(),
    )
    out_specs = (P("range", None, None), P("range", None, None), P(), P(), P())
    return jax.shard_map(
        on_device, mesh=mesh, in_specs=in_specs, out_specs=out_specs, check_vma=False
    )
```

```python
import math

import jax
import jax.numpy as jnp
from jax import lax
from jax.sharding import PartitionSpec as P

PX = 4
PY = 4
PZ = 8


def to_grid(slots):
    channels = slots.shape[-1]
    g = slots.reshape(2, 2, PX, PY, PZ, channels).transpose(0, 2, 1, 3, 4, 5)
    return g.reshape(2 * PX, 2 * PY, PZ, channels)


def from_grid(grid):
    channels = grid.shape[-1]
    g = grid.reshape(2, PX, 2, PY, PZ, channels).transpose(0, 2, 1, 3, 4, 5)
    return g.reshape(4, PX * PY * PZ, channels)


def padded_many(*grids):
    count = lax.axis_size("range")
    forward = [(i, i + 1) for i in range(count - 1)]
    backward = [(i + 1, i) for i in range(count - 1)]
    low = lax.ppermute(jnp.concatenate([g[:, :, PZ - 1 :] for g in grids], -1), "range", forward)
    high = lax.ppermute(jnp.concatenate([g[:, :, :1] for g in grids], -1), "range", backward)
    out = []
    for n, grid in enumerate(grids):
        width = grid.shape[-1]
        piece = slice(n * width, (n + 1) * width)
        wide = jnp.concatenate([low[..., piece], grid, high[..., piece]], axis=2)
        out.append(jnp.pad(wide, ((1, 1), (1, 1), (0, 0), (0, 0))))
    return out


def padded(grid):
    return padded_many(grid)[0]


def widened(depth, *grids):
    count = lax.axis_size("range")
    forward = [(i, i + 1) for i in range(count - 1)]
    backward = [(i + 1, i) for i in range(count - 1)]
    low = lax.ppermute(jnp.concatenate([g[:, :, PZ - depth :] for g in grids], -1), "range", forward)
    high = lax.ppermute(jnp.concatenate([g[:, :, :depth] for g in grids], -1), "range", backward)
    out = []
    for n, grid in enumerate(grids):
        width = grid.shape[-1]
        piece = slice(n * width, (n + 1) * width)
        out.append(jnp.concatenate([low[..., piece], grid, high[..., piece]], axis=2))
    return out


def xy_padded(grid):
    return jnp.pad(grid, ((1, 1), (1, 1), (0, 0), (0, 0)))


def z_columns_n(pad, planes):
    return jnp.concatenate([pad[:, :, sz : sz + planes] for sz in range(3)], axis=-1)


def z_columns(pad):
    return jnp.concatenate([pad[:, :, sz : sz + PZ] for sz in range(3)], axis=-1)


def xy_window(zcols, sx, sy):
    return zcols[sx : sx + 2 * PX, sy : sy + 2 * PY].reshape(-1, zcols.shape[-1])


def conv_apply(zcols, weights):
    channels = weights.shape[-1]
    taps = weights.reshape(3, 3, 3 * channels, channels)
    total = None
    for sx in range(3):
        for sy in range(3):
            term = jnp.dot(xy_window(zcols, sx, sy), taps[sx, sy], preferred_element_type=jnp.float32)
            total = term if total is None else total + term
    return total


def conv_weight_grad(zcols, upstream):
    contract_rows = (((0,), (0,)), ((), ()))
    terms = [
        lax.dot_general(xy_window(zcols, sx, sy), upstream, contract_rows, preferred_element_type=jnp.float32)
        for sx in range(3)
        for sy in range(3)
    ]
    return jnp.concatenate(terms, 0)

AXIS_SHIFT = {"y": 1, "x": 3, "z": 5}
PART_ORDERS = (("y", "x", "z"), ("x", "z", "y"), ("z", "y", "x"))


def coordinate(index, shift):
    return (index >> shift) & 3


def partner(index, shift, stage):
    c = (index >> shift) & 3
    other = c ^ 1 if stage == 0 else 3 - c
    return index + ((other - c) << shift)


def keep_bit(c, stage):
    if stage == 0:
        return ((c == 1) | (c == 2)).astype(jnp.int32)
    return (c >= 2).astype(jnp.int32)


def exchange_steps(order):
    return [(AXIS_SHIFT[axis], stage) for axis in order for stage in (0, 1)]


def split_halves(y, bit):
    h = y.shape[0] // 2
    keep = lax.dynamic_slice_in_dim(y, bit * h, h, 0)
    send = lax.dynamic_slice_in_dim(y, (1 - bit) * h, h, 0)
    return keep, send


def join_halves(y, got, bit):
    h = y.shape[0]
    full = jnp.zeros((2 * h,) + y.shape[1:], y.dtype)
    full = lax.dynamic_update_slice_in_dim(full, y, bit * h, 0)
    return lax.dynamic_update_slice_in_dim(full, got, (1 - bit) * h, 0)


def torus_psum(flat):
    count = lax.axis_size("range")
    index = lax.axis_index("range")
    core_perm = [(i, i ^ 1) for i in range(count)]
    core_bit = index & 1
    keep, send = split_halves(flat, core_bit)
    y = keep + lax.ppermute(send, "range", core_perm)
    parts = jnp.split(y, len(PART_ORDERS), 0)
    reduced = []
    for part, order in zip(parts, PART_ORDERS):
        for shift, stage in exchange_steps(order[:1]):
            perm = [(i, partner(i, shift, stage)) for i in range(count)]
            bit = keep_bit(coordinate(index, shift), stage)
            keep, send = split_halves(part, bit)
            part = keep + lax.ppermute(send, "range", perm)
        for shift, stage in exchange_steps(order[1:]):
            perm = [(i, partner(i, shift, stage)) for i in range(count)]
            part = part + lax.ppermute(part, "range", perm)
        reduced.append(part)
    gathered = []
    for part, order in zip(reduced, PART_ORDERS):
        part = part.astype(jnp.bfloat16)
        for shift, stage in reversed(exchange_steps(order[:1])):
            perm = [(i, partner(i, shift, stage)) for i in range(count)]
            bit = keep_bit(coordinate(index, shift), stage)
            part = join_halves(part, lax.ppermute(part, "range", perm), bit)
        gathered.append(part)
    y = jnp.concatenate(gathered, 0)
    return join_halves(y, lax.ppermute(y, "range", core_perm), core_bit).astype(jnp.float32)


def reversed_kernel(weights):
    taps = weights.shape[0]
    return jnp.concatenate([weights[taps - 1 - k][None] for k in range(taps)], 0).transpose(0, 2, 1)


def on_device(child_in, cotangent, child_of, neighbours, down_w, first_w, second_w):
    channels = child_in.shape[-1]
    kids_dev = child_in.shape[0]
    own_rank = lax.axis_index("range")
    f32 = jnp.float32
    bf16 = jnp.bfloat16

    slot_of = 2 * (neighbours[:, 4] >= 0).astype(jnp.int32) + (neighbours[:, 10] >= 0).astype(jnp.int32)
    match = slot_of[None, :] == jnp.arange(4, dtype=jnp.int32)[:, None]
    block_at = jnp.sum(jnp.where(match, jnp.arange(4, dtype=jnp.int32)[None, :], 0), axis=1)
    child_rows = child_of - own_rank * kids_dev
    fine_idx = child_rows[block_at].reshape(-1)
    inverse = jnp.zeros((kids_dev,), jnp.int32).at[fine_idx].set(jnp.arange(kids_dev, dtype=jnp.int32))

    fine = child_in[fine_idx].reshape(2, 2, 2, 2, 2, 2, 2, 2, 2, 4, 2, channels)
    patches = fine.transpose(0, 2, 5, 1, 3, 7, 4, 9, 6, 8, 10, 11).reshape(512, 8 * channels)
    down_flat = down_w.reshape(8 * channels, channels)
    hidden = jnp.dot(patches, down_flat, preferred_element_type=f32).astype(bf16)
    hidden_grid = hidden.reshape(2 * PX, 2 * PY, PZ, channels)

    cot_grid = to_grid(cotangent[block_at])
    cot_rows = cot_grid.reshape(-1, channels)
    hidden_wide, cot_wide = widened(2, hidden_grid, cot_grid)
    hidden_pad = xy_padded(hidden_wide)
    cot_pad = xy_padded(cot_wide)
    count = lax.axis_size("range")
    side_ok = jnp.stack([own_rank > 0, own_rank < count - 1]).reshape(2, 1, 1, 1)

    def halo_conv(pad, weights):
        sides = [jnp.concatenate([pad[:, :, t + sz] for sz in range(3)], -1) for t in (0, PZ + 1)]
        zc = jnp.stack(sides, 0)
        channels_out = weights.shape[-1]
        taps = weights.reshape(3, 3, -1, channels_out)
        total = None
        for sx in range(3):
            for sy in range(3):
                win = zc[:, sx : sx + 2 * PX, sy : sy + 2 * PY].reshape(-1, zc.shape[-1])
                term = jnp.dot(win, taps[sx, sy], preferred_element_type=f32)
                total = term if total is None else total + term
        return total.reshape(2, 2 * PX, 2 * PY, channels_out)

    def with_halo(own, halo):
        return jnp.concatenate([halo[0][:, :, None], own, halo[1][:, :, None]], axis=2)

    hidden_cols = z_columns(hidden_pad[:, :, 1 : PZ + 3])
    pre_act = conv_apply(hidden_cols, first_w)
    pre_halo = halo_conv(hidden_pad, first_w)
    act_own = jax.nn.silu(pre_act).astype(bf16).reshape(2 * PX, 2 * PY, PZ, channels)
    act_halo = jnp.where(side_ok, jax.nn.silu(pre_halo), 0.0).astype(bf16)
    act_cols = z_columns(xy_padded(with_halo(act_own, act_halo)))
    section = (
        hidden.astype(f32) + conv_apply(act_cols, second_w)
    ).astype(bf16)

    def d_pre_of(back, pre):
        sig = jax.nn.sigmoid(pre)
        return back * sig * (1.0 + pre * (1.0 - sig))

    cot_cols = z_columns(cot_pad[:, :, 1 : PZ + 3])
    back_act = conv_apply(cot_cols, reversed_kernel(second_w))
    back_halo = halo_conv(cot_pad, reversed_kernel(second_w))
    d_pre = d_pre_of(back_act, pre_act).astype(bf16)
    d_pre_halo = jnp.where(side_ok, d_pre_of(back_halo, pre_halo), 0.0).astype(bf16)
    d_pre_cols = z_columns(xy_padded(with_halo(d_pre.reshape(2 * PX, 2 * PY, PZ, channels), d_pre_halo)))
    d_hidden = (
        cot_rows.astype(f32)
        + conv_apply(d_pre_cols, reversed_kernel(first_w))
    ).astype(bf16)

    contract_rows = (((0,), (0,)), ((), ()))
    raw_first = conv_weight_grad(hidden_cols, d_pre)
    raw_second = conv_weight_grad(act_cols, cot_rows)
    raw_down = lax.dot_general(patches, d_hidden, contract_rows, preferred_element_type=f32)

    back = jnp.dot(d_hidden, down_flat.T, preferred_element_type=f32).astype(bf16)
    back = back.reshape(2, 2, 2, 2, 2, 2, 2, 4, 2, 2, 2, channels)
    back = back.transpose(0, 3, 1, 4, 6, 2, 8, 5, 9, 7, 10, 11).reshape(kids_dev, PX * PY * PZ, channels)
    child_grad = back[inverse]

    raw_grads = jnp.concatenate(
        [
            raw_down.reshape(8, channels, channels),
            raw_first.reshape(27, channels, channels),
            raw_second.reshape(27, channels, channels),
        ],
        0,
    )
    limit = jnp.float32(channels * math.sqrt(62.0))
    total_values = raw_grads.size
    rows = 8064
    flat = jnp.pad(raw_grads.reshape(-1), (0, rows * channels - total_values)).reshape(rows, channels)
    summed = torus_psum(flat).reshape(-1)[:total_values].reshape(raw_grads.shape)
    grad_total = jnp.sqrt(jnp.sum(summed * summed))
    clipped = summed * jnp.minimum(jnp.float32(1.0), limit / grad_total)
    section_out = from_grid(section.reshape(2 * PX, 2 * PY, PZ, channels))[slot_of]
    return (section_out, child_grad, clipped[:8], clipped[8:35], clipped[35:62])


def solution(mesh):
    in_specs = (
        P("range", None, None),
        P("range", None, None),
        P("range", None),
        P("range", None),
        P(),
        P(),
        P(),
    )
    out_specs = (P("range", None, None), P("range", None, None), P(), P(), P())
    return jax.shard_map(
        on_device, mesh=mesh, in_specs=in_specs, out_specs=out_specs, check_vma=False
    )
```

```python
import math

import jax
import jax.numpy as jnp
from jax import lax
from jax.sharding import PartitionSpec as P

PX = 4
PY = 4
PZ = 8


def to_grid(slots):
    channels = slots.shape[-1]
    g = slots.reshape(2, 2, PX, PY, PZ, channels).transpose(0, 2, 1, 3, 4, 5)
    return g.reshape(2 * PX, 2 * PY, PZ, channels)


def from_grid(grid):
    channels = grid.shape[-1]
    g = grid.reshape(2, PX, 2, PY, PZ, channels).transpose(0, 2, 1, 3, 4, 5)
    return g.reshape(4, PX * PY * PZ, channels)


def padded_many(*grids):
    count = lax.axis_size("range")
    forward = [(i, i + 1) for i in range(count - 1)]
    backward = [(i + 1, i) for i in range(count - 1)]
    low = lax.ppermute(jnp.concatenate([g[:, :, PZ - 1 :] for g in grids], -1), "range", forward)
    high = lax.ppermute(jnp.concatenate([g[:, :, :1] for g in grids], -1), "range", backward)
    out = []
    for n, grid in enumerate(grids):
        width = grid.shape[-1]
        piece = slice(n * width, (n + 1) * width)
        wide = jnp.concatenate([low[..., piece], grid, high[..., piece]], axis=2)
        out.append(jnp.pad(wide, ((1, 1), (1, 1), (0, 0), (0, 0))))
    return out


def padded(grid):
    return padded_many(grid)[0]


def widened(depth, *grids):
    count = lax.axis_size("range")
    forward = [(i, i + 1) for i in range(count - 1)]
    backward = [(i + 1, i) for i in range(count - 1)]
    low = lax.ppermute(jnp.concatenate([g[:, :, PZ - depth :] for g in grids], -1), "range", forward)
    high = lax.ppermute(jnp.concatenate([g[:, :, :depth] for g in grids], -1), "range", backward)
    out = []
    for n, grid in enumerate(grids):
        width = grid.shape[-1]
        piece = slice(n * width, (n + 1) * width)
        out.append(jnp.concatenate([low[..., piece], grid, high[..., piece]], axis=2))
    return out


def xy_padded(grid):
    return jnp.pad(grid, ((1, 1), (1, 1), (0, 0), (0, 0)))


def z_columns_n(pad, planes):
    return jnp.concatenate([pad[:, :, sz : sz + planes] for sz in range(3)], axis=-1)


def z_columns_reversed(pad):
    return jnp.concatenate([pad[:, :, sz : sz + PZ] for sz in (2, 1, 0)], axis=-1)


def conv_apply_reversed(zcols, weights):
    channels = weights.shape[-1]
    taps = weights.transpose(0, 2, 1).reshape(3, 3, 3 * channels, channels)
    total = None
    for sx in range(3):
        for sy in range(3):
            term = jnp.dot(xy_window(zcols, sx, sy), taps[2 - sx, 2 - sy], preferred_element_type=jnp.float32)
            total = term if total is None else total + term
    return total


def z_columns(pad):
    return jnp.concatenate([pad[:, :, sz : sz + PZ] for sz in range(3)], axis=-1)


def xy_window(zcols, sx, sy):
    return zcols[sx : sx + 2 * PX, sy : sy + 2 * PY].reshape(-1, zcols.shape[-1])


def conv_apply(zcols, weights):
    channels = weights.shape[-1]
    taps = weights.reshape(3, 3, 3 * channels, channels)
    total = None
    for sx in range(3):
        for sy in range(3):
            term = jnp.dot(xy_window(zcols, sx, sy), taps[sx, sy], preferred_element_type=jnp.float32)
            total = term if total is None else total + term
    return total


def conv_weight_grad(zcols, upstream):
    contract_rows = (((0,), (0,)), ((), ()))
    terms = [
        lax.dot_general(xy_window(zcols, sx, sy), upstream, contract_rows, preferred_element_type=jnp.float32)
        for sx in range(3)
        for sy in range(3)
    ]
    return jnp.concatenate(terms, 0)

AXIS_SHIFT = {"y": 1, "x": 3, "z": 5}
PART_ORDERS = (("y", "x", "z"), ("x", "z", "y"), ("z", "y", "x"))


def coordinate(index, shift):
    return (index >> shift) & 3


def partner(index, shift, stage):
    c = (index >> shift) & 3
    other = c ^ 1 if stage == 0 else 3 - c
    return index + ((other - c) << shift)


def keep_bit(c, stage):
    if stage == 0:
        return ((c == 1) | (c == 2)).astype(jnp.int32)
    return (c >= 2).astype(jnp.int32)


def exchange_steps(order):
    return [(AXIS_SHIFT[axis], stage) for axis in order for stage in (0, 1)]


def split_halves(y, bit):
    h = y.shape[0] // 2
    keep = lax.dynamic_slice_in_dim(y, bit * h, h, 0)
    send = lax.dynamic_slice_in_dim(y, (1 - bit) * h, h, 0)
    return keep, send


def join_halves(y, got, bit):
    h = y.shape[0]
    full = jnp.zeros((2 * h,) + y.shape[1:], y.dtype)
    full = lax.dynamic_update_slice_in_dim(full, y, bit * h, 0)
    return lax.dynamic_update_slice_in_dim(full, got, (1 - bit) * h, 0)


def torus_psum(flat):
    count = lax.axis_size("range")
    index = lax.axis_index("range")
    core_perm = [(i, i ^ 1) for i in range(count)]
    core_bit = index & 1
    keep, send = split_halves(flat, core_bit)
    y = keep + lax.ppermute(send, "range", core_perm)
    parts = jnp.split(y, len(PART_ORDERS), 0)
    reduced = []
    for part, order in zip(parts, PART_ORDERS):
        for shift, stage in exchange_steps(order[:1]):
            perm = [(i, partner(i, shift, stage)) for i in range(count)]
            bit = keep_bit(coordinate(index, shift), stage)
            keep, send = split_halves(part, bit)
            part = keep + lax.ppermute(send, "range", perm)
        for shift, stage in exchange_steps(order[1:]):
            perm = [(i, partner(i, shift, stage)) for i in range(count)]
            part = part + lax.ppermute(part, "range", perm)
        reduced.append(part)
    gathered = []
    for part, order in zip(reduced, PART_ORDERS):
        part = part.astype(jnp.bfloat16)
        for shift, stage in reversed(exchange_steps(order[:1])):
            perm = [(i, partner(i, shift, stage)) for i in range(count)]
            bit = keep_bit(coordinate(index, shift), stage)
            part = join_halves(part, lax.ppermute(part, "range", perm), bit)
        gathered.append(part)
    y = jnp.concatenate(gathered, 0)
    return join_halves(y, lax.ppermute(y, "range", core_perm), core_bit).astype(jnp.float32)


def reversed_kernel(weights):
    return jnp.flip(weights, 0).transpose(0, 2, 1)


def on_device(child_in, cotangent, child_of, neighbours, down_w, first_w, second_w):
    channels = child_in.shape[-1]
    kids_dev = child_in.shape[0]
    own_rank = lax.axis_index("range")
    f32 = jnp.float32
    bf16 = jnp.bfloat16

    slot_of = 2 * (neighbours[:, 4] >= 0).astype(jnp.int32) + (neighbours[:, 10] >= 0).astype(jnp.int32)
    match = slot_of[None, :] == jnp.arange(4, dtype=jnp.int32)[:, None]
    block_at = jnp.sum(jnp.where(match, jnp.arange(4, dtype=jnp.int32)[None, :], 0), axis=1)
    child_rows = child_of - own_rank * kids_dev
    fine_idx = child_rows[block_at].reshape(-1)
    inverse = jnp.zeros((kids_dev,), jnp.int32).at[fine_idx].set(jnp.arange(kids_dev, dtype=jnp.int32))

    fine = child_in[fine_idx].reshape(2, 2, 2, 2, 2, 2, 2, 2, 2, 4, 2, channels)
    patches = fine.transpose(0, 2, 5, 1, 3, 7, 4, 9, 6, 8, 10, 11).reshape(512, 8 * channels)
    down_flat = down_w.reshape(8 * channels, channels)
    hidden = jnp.dot(patches, down_flat, preferred_element_type=f32).astype(bf16)
    hidden_grid = hidden.reshape(2 * PX, 2 * PY, PZ, channels)

    cot_grid = to_grid(cotangent[block_at])
    cot_rows = cot_grid.reshape(-1, channels)
    hidden_wide, cot_wide = widened(2, hidden_grid, cot_grid)
    hidden_pad = xy_padded(hidden_wide)
    cot_pad = xy_padded(cot_wide)
    count = lax.axis_size("range")
    side_ok = jnp.stack([own_rank > 0, own_rank < count - 1]).reshape(2, 1, 1, 1)

    def halo_conv(pad, weights, reverse=False):
        order = (2, 1, 0) if reverse else (0, 1, 2)
        sides = [jnp.concatenate([pad[:, :, t + sz] for sz in order], -1) for t in (0, PZ + 1)]
        zc = jnp.stack(sides, 0)
        channels_out = weights.shape[-1]
        if reverse:
            taps = weights.transpose(0, 2, 1).reshape(3, 3, -1, channels_out)[::-1, ::-1]
        else:
            taps = weights.reshape(3, 3, -1, channels_out)
        total = None
        for sx in range(3):
            for sy in range(3):
                win = zc[:, sx : sx + 2 * PX, sy : sy + 2 * PY].reshape(-1, zc.shape[-1])
                term = jnp.dot(win, taps[sx, sy], preferred_element_type=f32)
                total = term if total is None else total + term
        return total.reshape(2, 2 * PX, 2 * PY, channels_out)

    def with_halo(own, halo):
        return jnp.concatenate([halo[0][:, :, None], own, halo[1][:, :, None]], axis=2)

    hidden_cols = z_columns(hidden_pad[:, :, 1 : PZ + 3])
    pre_act = conv_apply(hidden_cols, first_w)
    pre_halo = halo_conv(hidden_pad, first_w)
    act_own = jax.nn.silu(pre_act).astype(bf16).reshape(2 * PX, 2 * PY, PZ, channels)
    act_halo = jnp.where(side_ok, jax.nn.silu(pre_halo), 0.0).astype(bf16)
    act_cols = z_columns(xy_padded(with_halo(act_own, act_halo)))
    section = (
        hidden.astype(f32) + conv_apply(act_cols, second_w)
    ).astype(bf16)

    def d_pre_of(back, pre):
        sig = jax.nn.sigmoid(pre)
        return back * sig * (1.0 + pre * (1.0 - sig))

    cot_cols = z_columns_reversed(cot_pad[:, :, 1 : PZ + 3])
    back_act = conv_apply_reversed(cot_cols, second_w)
    back_halo = halo_conv(cot_pad, second_w, reverse=True)
    d_pre = d_pre_of(back_act, pre_act).astype(bf16)
    d_pre_halo = jnp.where(side_ok, d_pre_of(back_halo, pre_halo), 0.0).astype(bf16)
    d_pre_cols = z_columns_reversed(xy_padded(with_halo(d_pre.reshape(2 * PX, 2 * PY, PZ, channels), d_pre_halo)))
    d_hidden = (
        cot_rows.astype(f32)
        + conv_apply_reversed(d_pre_cols, first_w)
    ).astype(bf16)

    contract_rows = (((0,), (0,)), ((), ()))
    raw_first = conv_weight_grad(hidden_cols, d_pre)
    raw_second = conv_weight_grad(act_cols, cot_rows)
    raw_down = lax.dot_general(patches, d_hidden, contract_rows, preferred_element_type=f32)

    back = jnp.dot(d_hidden, down_flat.T, preferred_element_type=f32).astype(bf16)
    back = back.reshape(2, 2, 2, 2, 2, 2, 2, 4, 2, 2, 2, channels)
    back = back.transpose(0, 3, 1, 4, 6, 2, 8, 5, 9, 7, 10, 11).reshape(kids_dev, PX * PY * PZ, channels)
    child_grad = back[inverse]

    raw_grads = jnp.concatenate(
        [
            raw_down.reshape(8, channels, channels),
            raw_first.reshape(27, channels, channels),
            raw_second.reshape(27, channels, channels),
        ],
        0,
    )
    limit = jnp.float32(channels * math.sqrt(62.0))
    total_values = raw_grads.size
    rows = 8064
    flat = jnp.pad(raw_grads.reshape(-1), (0, rows * channels - total_values)).reshape(rows, channels)
    summed = torus_psum(flat).reshape(-1)[:total_values].reshape(raw_grads.shape)
    grad_total = jnp.sqrt(jnp.sum(summed * summed))
    clipped = summed * jnp.minimum(jnp.float32(1.0), limit / grad_total)
    section_out = from_grid(section.reshape(2 * PX, 2 * PY, PZ, channels))[slot_of]
    return (section_out, child_grad, clipped[:8], clipped[8:35], clipped[35:62])


def solution(mesh):
    in_specs = (
        P("range", None, None),
        P("range", None, None),
        P("range", None),
        P("range", None),
        P(),
        P(),
        P(),
    )
    out_specs = (P("range", None, None), P("range", None, None), P(), P(), P())
    return jax.shard_map(
        on_device, mesh=mesh, in_specs=in_specs, out_specs=out_specs, check_vma=False
    )
```

```python
import math

import jax
import jax.numpy as jnp
from jax import lax
from jax.sharding import PartitionSpec as P

PX = 4
PY = 4
PZ = 8


def to_grid(slots):
    channels = slots.shape[-1]
    g = slots.reshape(2, 2, PX, PY, PZ, channels).transpose(0, 2, 1, 3, 4, 5)
    return g.reshape(2 * PX, 2 * PY, PZ, channels)


def from_grid(grid):
    channels = grid.shape[-1]
    g = grid.reshape(2, PX, 2, PY, PZ, channels).transpose(0, 2, 1, 3, 4, 5)
    return g.reshape(4, PX * PY * PZ, channels)


def padded_many(*grids):
    count = lax.axis_size("range")
    forward = [(i, i + 1) for i in range(count - 1)]
    backward = [(i + 1, i) for i in range(count - 1)]
    low = lax.ppermute(jnp.concatenate([g[:, :, PZ - 1 :] for g in grids], -1), "range", forward)
    high = lax.ppermute(jnp.concatenate([g[:, :, :1] for g in grids], -1), "range", backward)
    out = []
    for n, grid in enumerate(grids):
        width = grid.shape[-1]
        piece = slice(n * width, (n + 1) * width)
        wide = jnp.concatenate([low[..., piece], grid, high[..., piece]], axis=2)
        out.append(jnp.pad(wide, ((1, 1), (1, 1), (0, 0), (0, 0))))
    return out


def padded(grid):
    return padded_many(grid)[0]


def widened(depth, *grids):
    count = lax.axis_size("range")
    forward = [(i, i + 1) for i in range(count - 1)]
    backward = [(i + 1, i) for i in range(count - 1)]
    low = lax.ppermute(jnp.concatenate([g[:, :, PZ - depth :] for g in grids], -1), "range", forward)
    high = lax.ppermute(jnp.concatenate([g[:, :, :depth] for g in grids], -1), "range", backward)
    out = []
    for n, grid in enumerate(grids):
        width = grid.shape[-1]
        piece = slice(n * width, (n + 1) * width)
        out.append(jnp.concatenate([low[..., piece], grid, high[..., piece]], axis=2))
    return out


def xy_padded(grid):
    return jnp.pad(grid, ((1, 1), (1, 1), (0, 0), (0, 0)))


def z_columns_n(pad, planes):
    return jnp.concatenate([pad[:, :, sz : sz + planes] for sz in range(3)], axis=-1)


def z_columns_reversed(pad):
    return jnp.concatenate([pad[:, :, sz : sz + PZ] for sz in (2, 1, 0)], axis=-1)


def conv_apply_reversed(zcols, weights):
    channels = weights.shape[-1]
    taps = weights.transpose(0, 2, 1).reshape(3, 3, 3 * channels, channels)
    total = None
    for sx in range(3):
        for sy in range(3):
            term = jnp.dot(xy_window(zcols, sx, sy), taps[2 - sx, 2 - sy], preferred_element_type=jnp.float32)
            total = term if total is None else total + term
    return total


def z_columns(pad):
    return jnp.concatenate([pad[:, :, sz : sz + PZ] for sz in range(3)], axis=-1)


def xy_window(zcols, sx, sy):
    return zcols[sx : sx + 2 * PX, sy : sy + 2 * PY].reshape(-1, zcols.shape[-1])


def conv_apply(zcols, weights):
    channels = weights.shape[-1]
    taps = weights.reshape(3, 3, 3 * channels, channels)
    total = None
    for sx in range(3):
        for sy in range(3):
            term = jnp.dot(xy_window(zcols, sx, sy), taps[sx, sy], preferred_element_type=jnp.float32)
            total = term if total is None else total + term
    return total


def conv_weight_grad(zcols, upstream):
    contract_rows = (((0,), (0,)), ((), ()))
    terms = [
        lax.dot_general(xy_window(zcols, sx, sy), upstream, contract_rows, preferred_element_type=jnp.float32)
        for sx in range(3)
        for sy in range(3)
    ]
    return jnp.concatenate(terms, 0)

AXIS_SHIFT = {"y": 1, "x": 3, "z": 5}
PART_ORDERS = (("y", "x", "z"), ("x", "z", "y"), ("z", "y", "x"))


def coordinate(index, shift):
    return (index >> shift) & 3


def partner(index, shift, stage):
    c = (index >> shift) & 3
    other = c ^ 1 if stage == 0 else 3 - c
    return index + ((other - c) << shift)


def keep_bit(c, stage):
    if stage == 0:
        return ((c == 1) | (c == 2)).astype(jnp.int32)
    return (c >= 2).astype(jnp.int32)


def exchange_steps(order):
    return [(AXIS_SHIFT[axis], stage) for axis in order for stage in (0, 1)]


def split_halves(y, bit):
    h = y.shape[0] // 2
    keep = lax.dynamic_slice_in_dim(y, bit * h, h, 0)
    send = lax.dynamic_slice_in_dim(y, (1 - bit) * h, h, 0)
    return keep, send


def join_halves(y, got, bit):
    h = y.shape[0]
    full = jnp.zeros((2 * h,) + y.shape[1:], y.dtype)
    full = lax.dynamic_update_slice_in_dim(full, y, bit * h, 0)
    return lax.dynamic_update_slice_in_dim(full, got, (1 - bit) * h, 0)


def torus_psum(flat):
    count = lax.axis_size("range")
    index = lax.axis_index("range")
    core_perm = [(i, i ^ 1) for i in range(count)]
    core_bit = index & 1
    keep, send = split_halves(flat, core_bit)
    y = keep + lax.ppermute(send, "range", core_perm)
    parts = jnp.split(y, len(PART_ORDERS), 0)
    reduced = []
    for part, order in zip(parts, PART_ORDERS):
        for shift, stage in exchange_steps(order[:1]):
            perm = [(i, partner(i, shift, stage)) for i in range(count)]
            bit = keep_bit(coordinate(index, shift), stage)
            keep, send = split_halves(part, bit)
            part = keep + lax.ppermute(send, "range", perm)
        for shift, stage in exchange_steps(order[1:]):
            perm = [(i, partner(i, shift, stage)) for i in range(count)]
            part = part + lax.ppermute(part, "range", perm)
        reduced.append(part)
    gathered = []
    for part, order in zip(reduced, PART_ORDERS):
        part = part.astype(jnp.bfloat16)
        for shift, stage in reversed(exchange_steps(order[:1])):
            perm = [(i, partner(i, shift, stage)) for i in range(count)]
            bit = keep_bit(coordinate(index, shift), stage)
            part = join_halves(part, lax.ppermute(part, "range", perm), bit)
        gathered.append(part)
    y = jnp.concatenate(gathered, 0)
    return join_halves(y, lax.ppermute(y, "range", core_perm), core_bit).astype(jnp.float32)


def reversed_kernel(weights):
    return jnp.flip(weights, 0).transpose(0, 2, 1)


def on_device(child_in, cotangent, child_of, neighbours, down_w, first_w, second_w):
    channels = child_in.shape[-1]
    kids_dev = child_in.shape[0]
    own_rank = lax.axis_index("range")
    f32 = jnp.float32
    bf16 = jnp.bfloat16

    slot_of = 2 * (neighbours[:, 4] >= 0).astype(jnp.int32) + (neighbours[:, 10] >= 0).astype(jnp.int32)
    match = slot_of[None, :] == jnp.arange(4, dtype=jnp.int32)[:, None]
    block_at = jnp.sum(jnp.where(match, jnp.arange(4, dtype=jnp.int32)[None, :], 0), axis=1)
    child_rows = child_of - own_rank * kids_dev
    fine_idx = child_rows[block_at].reshape(-1)
    inverse = jnp.zeros((kids_dev,), jnp.int32).at[fine_idx].set(jnp.arange(kids_dev, dtype=jnp.int32))

    fine = child_in[fine_idx].reshape(2, 2, 2, 2, 2, 2, 2, 2, 2, 4, 2, channels)
    patches = fine.transpose(0, 2, 5, 1, 3, 7, 4, 9, 6, 8, 10, 11).reshape(512, 8 * channels)
    down_flat = down_w.reshape(8 * channels, channels)
    hidden = jnp.dot(patches, down_flat, preferred_element_type=f32).astype(bf16)
    hidden_grid = hidden.reshape(2 * PX, 2 * PY, PZ, channels)

    cot_grid = to_grid(cotangent[block_at])
    cot_rows = cot_grid.reshape(-1, channels)
    hidden_wide, cot_wide = widened(2, hidden_grid, cot_grid)
    hidden_pad = xy_padded(hidden_wide)
    cot_pad = xy_padded(cot_wide)
    count = lax.axis_size("range")
    side_ok = jnp.stack([own_rank > 0, own_rank < count - 1]).reshape(2, 1, 1, 1)

    def halo_conv(pad, weights, reverse=False):
        order = (2, 1, 0) if reverse else (0, 1, 2)
        sides = [jnp.concatenate([pad[:, :, t + sz] for sz in order], -1) for t in (0, PZ + 1)]
        zc = jnp.stack(sides, 0)
        channels_out = weights.shape[-1]
        if reverse:
            taps = weights.transpose(0, 2, 1).reshape(3, 3, -1, channels_out)[::-1, ::-1]
        else:
            taps = weights.reshape(3, 3, -1, channels_out)
        total = None
        for sx in range(3):
            for sy in range(3):
                win = zc[:, sx : sx + 2 * PX, sy : sy + 2 * PY].reshape(-1, zc.shape[-1])
                term = jnp.dot(win, taps[sx, sy], preferred_element_type=f32)
                total = term if total is None else total + term
        return total.reshape(2, 2 * PX, 2 * PY, channels_out)

    def with_halo(own, halo):
        return jnp.concatenate([halo[0][:, :, None], own, halo[1][:, :, None]], axis=2)

    hidden_cols = z_columns(hidden_pad[:, :, 1 : PZ + 3])
    pre_act = conv_apply(hidden_cols, first_w)
    pre_halo = halo_conv(hidden_pad, first_w)
    act_own = jax.nn.silu(pre_act).astype(bf16).reshape(2 * PX, 2 * PY, PZ, channels)
    act_halo = jnp.where(side_ok, jax.nn.silu(pre_halo), 0.0).astype(bf16)
    act_cols = z_columns(xy_padded(with_halo(act_own, act_halo)))
    section = (
        hidden.astype(f32) + conv_apply(act_cols, second_w)
    ).astype(bf16)

    def d_pre_of(back, pre):
        sig = jax.nn.sigmoid(pre)
        return back * sig * (1.0 + pre * (1.0 - sig))

    cot_cols = z_columns_reversed(cot_pad[:, :, 1 : PZ + 3])
    back_act = conv_apply_reversed(cot_cols, second_w)
    back_halo = halo_conv(cot_pad, second_w, reverse=True)
    d_pre = d_pre_of(back_act, pre_act).astype(bf16)
    d_pre_halo = jnp.where(side_ok, d_pre_of(back_halo, pre_halo), 0.0).astype(bf16)
    d_pre_cols = z_columns_reversed(xy_padded(with_halo(d_pre.reshape(2 * PX, 2 * PY, PZ, channels), d_pre_halo)))
    d_hidden = (
        cot_rows.astype(f32)
        + conv_apply_reversed(d_pre_cols, first_w)
    ).astype(bf16)

    contract_rows = (((0,), (0,)), ((), ()))
    raw_first = conv_weight_grad(hidden_cols, d_pre)
    raw_second = conv_weight_grad(act_cols, cot_rows)
    raw_down = lax.dot_general(patches, d_hidden, contract_rows, preferred_element_type=f32)

    back = jnp.dot(d_hidden, down_flat.T, preferred_element_type=f32).astype(bf16)
    back = back.reshape(2, 2, 2, 2, 2, 2, 2, 4, 2, 2, 2, channels)
    back = back.transpose(0, 3, 1, 4, 6, 2, 8, 5, 9, 7, 10, 11).reshape(kids_dev, PX * PY * PZ, channels)
    child_grad = back[inverse]

    raw_grads = jnp.concatenate(
        [
            raw_down.reshape(8, channels, channels),
            raw_first.reshape(27, channels, channels),
            raw_second.reshape(27, channels, channels),
        ],
        0,
    )
    limit = jnp.float32(channels * math.sqrt(62.0))
    total_values = raw_grads.size
    rows = 8064
    flat = jnp.pad(raw_grads.reshape(-1), (0, rows * channels - total_values)).reshape(rows, channels)
    summed = torus_psum(flat).reshape(-1)[:total_values].reshape(raw_grads.shape)
    partial = jnp.sum((summed * summed).reshape(summed.shape[0], -1), axis=1)
    grad_total = jnp.sqrt(jnp.sum(lax.optimization_barrier(partial)))
    clipped = summed * jnp.minimum(jnp.float32(1.0), limit / grad_total)
    section_out = from_grid(section.reshape(2 * PX, 2 * PY, PZ, channels))[slot_of]
    return (section_out, child_grad, clipped[:8], clipped[8:35], clipped[35:62])


def solution(mesh):
    in_specs = (
        P("range", None, None),
        P("range", None, None),
        P("range", None),
        P("range", None),
        P(),
        P(),
        P(),
    )
    out_specs = (P("range", None, None), P("range", None, None), P(), P(), P())
    return jax.shard_map(
        on_device, mesh=mesh, in_specs=in_specs, out_specs=out_specs, check_vma=False
    )
```

```python
import math

import jax
import jax.numpy as jnp
from jax import lax
from jax.sharding import PartitionSpec as P

PX = 4
PY = 4
PZ = 8


def to_grid(slots):
    channels = slots.shape[-1]
    g = slots.reshape(2, 2, PX, PY, PZ, channels).transpose(0, 2, 1, 3, 4, 5)
    return g.reshape(2 * PX, 2 * PY, PZ, channels)


def from_grid(grid):
    channels = grid.shape[-1]
    g = grid.reshape(2, PX, 2, PY, PZ, channels).transpose(0, 2, 1, 3, 4, 5)
    return g.reshape(4, PX * PY * PZ, channels)


def padded_many(*grids):
    count = lax.axis_size("range")
    forward = [(i, i + 1) for i in range(count - 1)]
    backward = [(i + 1, i) for i in range(count - 1)]
    low = lax.ppermute(jnp.concatenate([g[:, :, PZ - 1 :] for g in grids], -1), "range", forward)
    high = lax.ppermute(jnp.concatenate([g[:, :, :1] for g in grids], -1), "range", backward)
    out = []
    for n, grid in enumerate(grids):
        width = grid.shape[-1]
        piece = slice(n * width, (n + 1) * width)
        wide = jnp.concatenate([low[..., piece], grid, high[..., piece]], axis=2)
        out.append(jnp.pad(wide, ((1, 1), (1, 1), (0, 0), (0, 0))))
    return out


def padded(grid):
    return padded_many(grid)[0]


def widened(depth, *grids):
    count = lax.axis_size("range")
    forward = [(i, i + 1) for i in range(count - 1)]
    backward = [(i + 1, i) for i in range(count - 1)]
    low = lax.ppermute(jnp.concatenate([g[:, :, PZ - depth :] for g in grids], -1), "range", forward)
    high = lax.ppermute(jnp.concatenate([g[:, :, :depth] for g in grids], -1), "range", backward)
    out = []
    for n, grid in enumerate(grids):
        width = grid.shape[-1]
        piece = slice(n * width, (n + 1) * width)
        out.append(jnp.concatenate([low[..., piece], grid, high[..., piece]], axis=2))
    return out


def xy_padded(grid):
    return jnp.pad(grid, ((1, 1), (1, 1), (0, 0), (0, 0)))


def z_columns_n(pad, planes):
    return jnp.concatenate([pad[:, :, sz : sz + planes] for sz in range(3)], axis=-1)


def z_columns_reversed(pad):
    return jnp.concatenate([pad[:, :, sz : sz + PZ] for sz in (2, 1, 0)], axis=-1)


def conv_apply_reversed(zcols, weights):
    channels = weights.shape[-1]
    taps = weights.transpose(0, 2, 1).reshape(3, 3, 3 * channels, channels)
    total = None
    for sx in range(3):
        for sy in range(3):
            term = jnp.dot(xy_window(zcols, sx, sy), taps[2 - sx, 2 - sy], preferred_element_type=jnp.float32)
            total = term if total is None else total + term
    return total


def z_columns(pad):
    return jnp.concatenate([pad[:, :, sz : sz + PZ] for sz in range(3)], axis=-1)


def xy_window(zcols, sx, sy):
    return zcols[sx : sx + 2 * PX, sy : sy + 2 * PY].reshape(-1, zcols.shape[-1])


def conv_apply(zcols, weights):
    channels = weights.shape[-1]
    taps = weights.reshape(3, 3, 3 * channels, channels)
    total = None
    for sx in range(3):
        for sy in range(3):
            term = jnp.dot(xy_window(zcols, sx, sy), taps[sx, sy], preferred_element_type=jnp.float32)
            total = term if total is None else total + term
    return total


def conv_weight_grad(zcols, upstream):
    contract_rows = (((0,), (0,)), ((), ()))
    terms = [
        lax.dot_general(xy_window(zcols, sx, sy), upstream, contract_rows, preferred_element_type=jnp.float32)
        for sx in range(3)
        for sy in range(3)
    ]
    return jnp.concatenate(terms, 0)

AXIS_SHIFT = {"y": 1, "x": 3, "z": 5}
PART_ORDERS = (("y", "x", "z"), ("x", "z", "y"), ("z", "y", "x"))


def coordinate(index, shift):
    return (index >> shift) & 3


def partner(index, shift, stage):
    c = (index >> shift) & 3
    other = c ^ 1 if stage == 0 else 3 - c
    return index + ((other - c) << shift)


def keep_bit(c, stage):
    if stage == 0:
        return ((c == 1) | (c == 2)).astype(jnp.int32)
    return (c >= 2).astype(jnp.int32)


def exchange_steps(order):
    return [(AXIS_SHIFT[axis], stage) for axis in order for stage in (0, 1)]


def split_halves(y, bit):
    h = y.shape[0] // 2
    keep = lax.dynamic_slice_in_dim(y, bit * h, h, 0)
    send = lax.dynamic_slice_in_dim(y, (1 - bit) * h, h, 0)
    return keep, send


def join_halves(y, got, bit):
    h = y.shape[0]
    full = jnp.zeros((2 * h,) + y.shape[1:], y.dtype)
    full = lax.dynamic_update_slice_in_dim(full, y, bit * h, 0)
    return lax.dynamic_update_slice_in_dim(full, got, (1 - bit) * h, 0)


def torus_psum(flat, late=()):
    count = lax.axis_size("range")
    index = lax.axis_index("range")
    core_perm = [(i, i ^ 1) for i in range(count)]
    core_bit = index & 1
    keep, send = split_halves(flat, core_bit)
    y = keep + lax.ppermute(send, "range", core_perm)
    y, late = lax.optimization_barrier((y, late))
    parts = jnp.split(y, len(PART_ORDERS), 0)
    reduced = []
    for part, order in zip(parts, PART_ORDERS):
        for shift, stage in exchange_steps(order[:1]):
            perm = [(i, partner(i, shift, stage)) for i in range(count)]
            bit = keep_bit(coordinate(index, shift), stage)
            keep, send = split_halves(part, bit)
            part = keep + lax.ppermute(send, "range", perm)
        for shift, stage in exchange_steps(order[1:]):
            perm = [(i, partner(i, shift, stage)) for i in range(count)]
            part = part + lax.ppermute(part, "range", perm)
        reduced.append(part)
    gathered = []
    for part, order in zip(reduced, PART_ORDERS):
        part = part.astype(jnp.bfloat16)
        for shift, stage in reversed(exchange_steps(order[:1])):
            perm = [(i, partner(i, shift, stage)) for i in range(count)]
            bit = keep_bit(coordinate(index, shift), stage)
            part = join_halves(part, lax.ppermute(part, "range", perm), bit)
        gathered.append(part)
    y = jnp.concatenate(gathered, 0)
    return join_halves(y, lax.ppermute(y, "range", core_perm), core_bit).astype(jnp.float32), late


def reversed_kernel(weights):
    return jnp.flip(weights, 0).transpose(0, 2, 1)


def on_device(child_in, cotangent, child_of, neighbours, down_w, first_w, second_w):
    channels = child_in.shape[-1]
    kids_dev = child_in.shape[0]
    own_rank = lax.axis_index("range")
    f32 = jnp.float32
    bf16 = jnp.bfloat16

    slot_of = 2 * (neighbours[:, 4] >= 0).astype(jnp.int32) + (neighbours[:, 10] >= 0).astype(jnp.int32)
    match = slot_of[None, :] == jnp.arange(4, dtype=jnp.int32)[:, None]
    block_at = jnp.sum(jnp.where(match, jnp.arange(4, dtype=jnp.int32)[None, :], 0), axis=1)
    child_rows = child_of - own_rank * kids_dev
    fine_idx = child_rows[block_at].reshape(-1)
    inverse = jnp.zeros((kids_dev,), jnp.int32).at[fine_idx].set(jnp.arange(kids_dev, dtype=jnp.int32))

    fine = child_in[fine_idx].reshape(2, 2, 2, 2, 2, 2, 2, 2, 2, 4, 2, channels)
    patches = fine.transpose(0, 2, 5, 1, 3, 7, 4, 9, 6, 8, 10, 11).reshape(512, 8 * channels)
    down_flat = down_w.reshape(8 * channels, channels)
    hidden = jnp.dot(patches, down_flat, preferred_element_type=f32).astype(bf16)
    hidden_grid = hidden.reshape(2 * PX, 2 * PY, PZ, channels)

    cot_grid = to_grid(cotangent[block_at])
    cot_rows = cot_grid.reshape(-1, channels)
    hidden_wide, cot_wide = widened(2, hidden_grid, cot_grid)
    hidden_pad = xy_padded(hidden_wide)
    cot_pad = xy_padded(cot_wide)
    count = lax.axis_size("range")
    side_ok = jnp.stack([own_rank > 0, own_rank < count - 1]).reshape(2, 1, 1, 1)

    def halo_conv(pad, weights, reverse=False):
        order = (2, 1, 0) if reverse else (0, 1, 2)
        sides = [jnp.concatenate([pad[:, :, t + sz] for sz in order], -1) for t in (0, PZ + 1)]
        zc = jnp.stack(sides, 0)
        channels_out = weights.shape[-1]
        if reverse:
            taps = weights.transpose(0, 2, 1).reshape(3, 3, -1, channels_out)[::-1, ::-1]
        else:
            taps = weights.reshape(3, 3, -1, channels_out)
        total = None
        for sx in range(3):
            for sy in range(3):
                win = zc[:, sx : sx + 2 * PX, sy : sy + 2 * PY].reshape(-1, zc.shape[-1])
                term = jnp.dot(win, taps[sx, sy], preferred_element_type=f32)
                total = term if total is None else total + term
        return total.reshape(2, 2 * PX, 2 * PY, channels_out)

    def with_halo(own, halo):
        return jnp.concatenate([halo[0][:, :, None], own, halo[1][:, :, None]], axis=2)

    hidden_cols = z_columns(hidden_pad[:, :, 1 : PZ + 3])
    pre_act = conv_apply(hidden_cols, first_w)
    pre_halo = halo_conv(hidden_pad, first_w)
    act_own = jax.nn.silu(pre_act).astype(bf16).reshape(2 * PX, 2 * PY, PZ, channels)
    act_halo = jnp.where(side_ok, jax.nn.silu(pre_halo), 0.0).astype(bf16)
    act_cols = z_columns(xy_padded(with_halo(act_own, act_halo)))

    def d_pre_of(back, pre):
        sig = jax.nn.sigmoid(pre)
        return back * sig * (1.0 + pre * (1.0 - sig))

    cot_cols = z_columns_reversed(cot_pad[:, :, 1 : PZ + 3])
    back_act = conv_apply_reversed(cot_cols, second_w)
    back_halo = halo_conv(cot_pad, second_w, reverse=True)
    d_pre = d_pre_of(back_act, pre_act).astype(bf16)
    d_pre_halo = jnp.where(side_ok, d_pre_of(back_halo, pre_halo), 0.0).astype(bf16)
    d_pre_cols = z_columns_reversed(xy_padded(with_halo(d_pre.reshape(2 * PX, 2 * PY, PZ, channels), d_pre_halo)))
    d_hidden = (
        cot_rows.astype(f32)
        + conv_apply_reversed(d_pre_cols, first_w)
    ).astype(bf16)

    contract_rows = (((0,), (0,)), ((), ()))
    raw_first = conv_weight_grad(hidden_cols, d_pre)
    raw_second = conv_weight_grad(act_cols, cot_rows)
    raw_down = lax.dot_general(patches, d_hidden, contract_rows, preferred_element_type=f32)

    back = jnp.dot(d_hidden, down_flat.T, preferred_element_type=f32).astype(bf16)
    back = back.reshape(2, 2, 2, 2, 2, 2, 2, 4, 2, 2, 2, channels)
    back = back.transpose(0, 3, 1, 4, 6, 2, 8, 5, 9, 7, 10, 11).reshape(kids_dev, PX * PY * PZ, channels)
    child_grad = back[inverse]

    raw_grads = jnp.concatenate(
        [
            raw_down.reshape(8, channels, channels),
            raw_first.reshape(27, channels, channels),
            raw_second.reshape(27, channels, channels),
        ],
        0,
    )
    limit = jnp.float32(channels * math.sqrt(62.0))
    total_values = raw_grads.size
    rows = 8064
    flat = jnp.pad(raw_grads.reshape(-1), (0, rows * channels - total_values)).reshape(rows, channels)
    summed, (late_cols, late_hidden) = torus_psum(flat, (act_cols, hidden))
    summed = summed.reshape(-1)[:total_values].reshape(raw_grads.shape)
    section = (late_hidden.astype(f32) + conv_apply(late_cols, second_w)).astype(bf16)
    partial = jnp.sum((summed * summed).reshape(summed.shape[0], -1), axis=1)
    grad_total = jnp.sqrt(jnp.sum(lax.optimization_barrier(partial)))
    clipped = summed * jnp.minimum(jnp.float32(1.0), limit / grad_total)
    section_out = from_grid(section.reshape(2 * PX, 2 * PY, PZ, channels))[slot_of]
    return (section_out, child_grad, clipped[:8], clipped[8:35], clipped[35:62])


def solution(mesh):
    in_specs = (
        P("range", None, None),
        P("range", None, None),
        P("range", None),
        P("range", None),
        P(),
        P(),
        P(),
    )
    out_specs = (P("range", None, None), P("range", None, None), P(), P(), P())
    return jax.shard_map(
        on_device, mesh=mesh, in_specs=in_specs, out_specs=out_specs, check_vma=False
    )
```

```python
import math

import jax
import jax.numpy as jnp
from jax import lax
from jax.sharding import PartitionSpec as P

PX = 4
PY = 4
PZ = 8


def to_grid(slots):
    channels = slots.shape[-1]
    g = slots.reshape(2, 2, PX, PY, PZ, channels).transpose(0, 2, 1, 3, 4, 5)
    return g.reshape(2 * PX, 2 * PY, PZ, channels)


def from_grid(grid):
    channels = grid.shape[-1]
    g = grid.reshape(2, PX, 2, PY, PZ, channels).transpose(0, 2, 1, 3, 4, 5)
    return g.reshape(4, PX * PY * PZ, channels)


def padded_many(*grids):
    count = lax.axis_size("range")
    forward = [(i, i + 1) for i in range(count - 1)]
    backward = [(i + 1, i) for i in range(count - 1)]
    low = lax.ppermute(jnp.concatenate([g[:, :, PZ - 1 :] for g in grids], -1), "range", forward)
    high = lax.ppermute(jnp.concatenate([g[:, :, :1] for g in grids], -1), "range", backward)
    out = []
    for n, grid in enumerate(grids):
        width = grid.shape[-1]
        piece = slice(n * width, (n + 1) * width)
        wide = jnp.concatenate([low[..., piece], grid, high[..., piece]], axis=2)
        out.append(jnp.pad(wide, ((1, 1), (1, 1), (0, 0), (0, 0))))
    return out


def padded(grid):
    return padded_many(grid)[0]


def widened(depth, *grids):
    count = lax.axis_size("range")
    forward = [(i, i + 1) for i in range(count - 1)]
    backward = [(i + 1, i) for i in range(count - 1)]
    low = lax.ppermute(jnp.concatenate([g[:, :, PZ - depth :] for g in grids], -1), "range", forward)
    high = lax.ppermute(jnp.concatenate([g[:, :, :depth] for g in grids], -1), "range", backward)
    out = []
    for n, grid in enumerate(grids):
        width = grid.shape[-1]
        piece = slice(n * width, (n + 1) * width)
        out.append(jnp.concatenate([low[..., piece], grid, high[..., piece]], axis=2))
    return out


def xy_padded(grid):
    return jnp.pad(grid, ((1, 1), (1, 1), (0, 0), (0, 0)))


def z_columns_n(pad, planes):
    return jnp.concatenate([pad[:, :, sz : sz + planes] for sz in range(3)], axis=-1)


def z_columns_reversed(pad):
    return jnp.concatenate([pad[:, :, sz : sz + PZ] for sz in (2, 1, 0)], axis=-1)


def conv_apply_reversed(zcols, weights):
    channels = weights.shape[-1]
    taps = weights.transpose(0, 2, 1).reshape(3, 3, 3 * channels, channels)
    total = None
    for sx in range(3):
        for sy in range(3):
            term = jnp.dot(xy_window(zcols, sx, sy), taps[2 - sx, 2 - sy], preferred_element_type=jnp.float32)
            total = term if total is None else total + term
    return total


def z_columns(pad):
    return jnp.concatenate([pad[:, :, sz : sz + PZ] for sz in range(3)], axis=-1)


def xy_window(zcols, sx, sy):
    return zcols[sx : sx + 2 * PX, sy : sy + 2 * PY].reshape(-1, zcols.shape[-1])


def conv_apply(zcols, weights):
    channels = weights.shape[-1]
    taps = weights.reshape(3, 3, 3 * channels, channels)
    total = None
    for sx in range(3):
        for sy in range(3):
            term = jnp.dot(xy_window(zcols, sx, sy), taps[sx, sy], preferred_element_type=jnp.float32)
            total = term if total is None else total + term
    return total


def conv_weight_grad(zcols, upstream):
    contract_rows = (((0,), (0,)), ((), ()))
    terms = [
        lax.dot_general(xy_window(zcols, sx, sy), upstream, contract_rows, preferred_element_type=jnp.float32)
        for sx in range(3)
        for sy in range(3)
    ]
    return jnp.concatenate(terms, 0)

AXIS_SHIFT = {"y": 1, "x": 3, "z": 5}
PART_ORDERS = (("y", "x", "z"), ("x", "z", "y"), ("z", "y", "x"))


def coordinate(index, shift):
    return (index >> shift) & 3


def partner(index, shift, stage):
    c = (index >> shift) & 3
    other = c ^ 1 if stage == 0 else 3 - c
    return index + ((other - c) << shift)


def keep_bit(c, stage):
    if stage == 0:
        return ((c == 1) | (c == 2)).astype(jnp.int32)
    return (c >= 2).astype(jnp.int32)


def exchange_steps(order):
    return [(AXIS_SHIFT[axis], stage) for axis in order for stage in (0, 1)]


def split_halves(y, bit):
    h = y.shape[0] // 2
    keep = lax.dynamic_slice_in_dim(y, bit * h, h, 0)
    send = lax.dynamic_slice_in_dim(y, (1 - bit) * h, h, 0)
    return keep, send


def join_halves(y, got, bit):
    h = y.shape[0]
    full = jnp.zeros((2 * h,) + y.shape[1:], y.dtype)
    full = lax.dynamic_update_slice_in_dim(full, y, bit * h, 0)
    return lax.dynamic_update_slice_in_dim(full, got, (1 - bit) * h, 0)


def torus_psum(flat, late=()):
    count = lax.axis_size("range")
    index = lax.axis_index("range")
    core_perm = [(i, i ^ 1) for i in range(count)]
    core_bit = index & 1
    keep, send = split_halves(flat, core_bit)
    y = keep + lax.ppermute(send, "range", core_perm)
    y, late = lax.optimization_barrier((y, late))
    parts = jnp.split(y, len(PART_ORDERS), 0)
    reduced = []
    for part, order in zip(parts, PART_ORDERS):
        for shift, stage in exchange_steps(order[:1]):
            perm = [(i, partner(i, shift, stage)) for i in range(count)]
            bit = keep_bit(coordinate(index, shift), stage)
            keep, send = split_halves(part, bit)
            part = keep + lax.ppermute(send, "range", perm)
        for shift, stage in exchange_steps(order[1:]):
            perm = [(i, partner(i, shift, stage)) for i in range(count)]
            part = part + lax.ppermute(part, "range", perm)
        reduced.append(part)
    gathered = []
    for part, order in zip(reduced, PART_ORDERS):
        part = part.astype(jnp.bfloat16)
        for shift, stage in reversed(exchange_steps(order[:1])):
            perm = [(i, partner(i, shift, stage)) for i in range(count)]
            bit = keep_bit(coordinate(index, shift), stage)
            part = join_halves(part, lax.ppermute(part, "range", perm), bit)
        gathered.append(part)
    y = jnp.concatenate(gathered, 0)
    return join_halves(y, lax.ppermute(y, "range", core_perm), core_bit).astype(jnp.float32), late


def reversed_kernel(weights):
    return jnp.flip(weights, 0).transpose(0, 2, 1)


def on_device(child_in, cotangent, child_of, neighbours, down_w, first_w, second_w):
    channels = child_in.shape[-1]
    kids_dev = child_in.shape[0]
    own_rank = lax.axis_index("range")
    f32 = jnp.float32
    bf16 = jnp.bfloat16

    slot_of = 2 * (neighbours[:, 4] >= 0).astype(jnp.int32) + (neighbours[:, 10] >= 0).astype(jnp.int32)
    match = slot_of[None, :] == jnp.arange(4, dtype=jnp.int32)[:, None]
    block_at = jnp.sum(jnp.where(match, jnp.arange(4, dtype=jnp.int32)[None, :], 0), axis=1)
    child_rows = child_of - own_rank * kids_dev
    fine_idx = child_rows[block_at].reshape(-1)
    inverse = jnp.zeros((kids_dev,), jnp.int32).at[fine_idx].set(jnp.arange(kids_dev, dtype=jnp.int32))

    fine = child_in[fine_idx].reshape(2, 2, 2, 2, 2, 2, 2, 2, 2, 4, 2, channels)
    patches = fine.transpose(0, 2, 5, 1, 3, 7, 4, 9, 6, 8, 10, 11).reshape(512, 8 * channels)
    down_flat = down_w.reshape(8 * channels, channels)
    hidden = jnp.dot(patches, down_flat, preferred_element_type=f32).astype(bf16)
    hidden_grid = hidden.reshape(2 * PX, 2 * PY, PZ, channels)

    cot_grid = to_grid(cotangent[block_at])
    cot_rows = cot_grid.reshape(-1, channels)
    hidden_wide, cot_wide = widened(2, hidden_grid, cot_grid)
    hidden_pad = xy_padded(hidden_wide)
    cot_pad = xy_padded(cot_wide)
    count = lax.axis_size("range")
    side_ok = jnp.stack([own_rank > 0, own_rank < count - 1]).reshape(2, 1, 1, 1)

    def halo_conv(pad, weights, reverse=False):
        order = (2, 1, 0) if reverse else (0, 1, 2)
        sides = [jnp.concatenate([pad[:, :, t + sz] for sz in order], -1) for t in (0, PZ + 1)]
        zc = jnp.stack(sides, 0)
        channels_out = weights.shape[-1]
        if reverse:
            taps = weights.transpose(0, 2, 1).reshape(3, 3, -1, channels_out)[::-1, ::-1]
        else:
            taps = weights.reshape(3, 3, -1, channels_out)
        total = None
        for sx in range(3):
            for sy in range(3):
                win = zc[:, sx : sx + 2 * PX, sy : sy + 2 * PY].reshape(-1, zc.shape[-1])
                term = jnp.dot(win, taps[sx, sy], preferred_element_type=f32)
                total = term if total is None else total + term
        return total.reshape(2, 2 * PX, 2 * PY, channels_out)

    def with_halo(own, halo):
        return jnp.concatenate([halo[0][:, :, None], own, halo[1][:, :, None]], axis=2)

    hidden_cols = z_columns(hidden_pad[:, :, 1 : PZ + 3])
    pre_act = conv_apply(hidden_cols, first_w)
    pre_halo = halo_conv(hidden_pad, first_w)
    act_own = jax.nn.silu(pre_act).astype(bf16).reshape(2 * PX, 2 * PY, PZ, channels)
    act_halo = jnp.where(side_ok, jax.nn.silu(pre_halo), 0.0).astype(bf16)
    act_cols = z_columns(xy_padded(with_halo(act_own, act_halo)))

    def d_pre_of(back, pre):
        sig = jax.nn.sigmoid(pre)
        return back * sig * (1.0 + pre * (1.0 - sig))

    cot_cols = z_columns_reversed(cot_pad[:, :, 1 : PZ + 3])
    back_act = conv_apply_reversed(cot_cols, second_w)
    back_halo = halo_conv(cot_pad, second_w, reverse=True)
    d_pre = d_pre_of(back_act, pre_act).astype(bf16)
    d_pre_halo = jnp.where(side_ok, d_pre_of(back_halo, pre_halo), 0.0).astype(bf16)
    d_pre_cols = z_columns_reversed(xy_padded(with_halo(d_pre.reshape(2 * PX, 2 * PY, PZ, channels), d_pre_halo)))
    d_hidden = (
        cot_rows.astype(f32)
        + conv_apply_reversed(d_pre_cols, first_w)
    ).astype(bf16)

    contract_rows = (((0,), (0,)), ((), ()))
    raw_first = conv_weight_grad(hidden_cols, d_pre)
    raw_second = conv_weight_grad(act_cols, cot_rows)
    raw_down = lax.dot_general(patches, d_hidden, contract_rows, preferred_element_type=f32)


    raw_grads = jnp.concatenate(
        [
            raw_down.reshape(8, channels, channels),
            raw_first.reshape(27, channels, channels),
            raw_second.reshape(27, channels, channels),
        ],
        0,
    )
    limit = jnp.float32(channels * math.sqrt(62.0))
    total_values = raw_grads.size
    rows = 8064
    flat = jnp.pad(raw_grads.reshape(-1), (0, rows * channels - total_values)).reshape(rows, channels)
    summed, (late_cols, late_hidden, late_d_hidden) = torus_psum(flat, (act_cols, hidden, d_hidden))
    back = jnp.dot(late_d_hidden, down_flat.T, preferred_element_type=f32).astype(bf16)
    back = back.reshape(2, 2, 2, 2, 2, 2, 2, 4, 2, 2, 2, channels)
    back = back.transpose(0, 3, 1, 4, 6, 2, 8, 5, 9, 7, 10, 11).reshape(kids_dev, PX * PY * PZ, channels)
    child_grad = back[inverse]
    summed = summed.reshape(-1)[:total_values].reshape(raw_grads.shape)
    section = (late_hidden.astype(f32) + conv_apply(late_cols, second_w)).astype(bf16)
    partial = jnp.sum((summed * summed).reshape(summed.shape[0], -1), axis=1)
    grad_total = jnp.sqrt(jnp.sum(lax.optimization_barrier(partial)))
    clipped = summed * jnp.minimum(jnp.float32(1.0), limit / grad_total)
    section_out = from_grid(section.reshape(2 * PX, 2 * PY, PZ, channels))[slot_of]
    return (section_out, child_grad, clipped[:8], clipped[8:35], clipped[35:62])


def solution(mesh):
    in_specs = (
        P("range", None, None),
        P("range", None, None),
        P("range", None),
        P("range", None),
        P(),
        P(),
        P(),
    )
    out_specs = (P("range", None, None), P("range", None, None), P(), P(), P())
    return jax.shard_map(
        on_device, mesh=mesh, in_specs=in_specs, out_specs=out_specs, check_vma=False
    )
```

```python
import math

import jax
import jax.numpy as jnp
from jax import lax
from jax.sharding import PartitionSpec as P

PX = 4
PY = 4
PZ = 8


def to_grid(slots):
    channels = slots.shape[-1]
    g = slots.reshape(2, 2, PX, PY, PZ, channels).transpose(0, 2, 1, 3, 4, 5)
    return g.reshape(2 * PX, 2 * PY, PZ, channels)


def from_grid(grid):
    channels = grid.shape[-1]
    g = grid.reshape(2, PX, 2, PY, PZ, channels).transpose(0, 2, 1, 3, 4, 5)
    return g.reshape(4, PX * PY * PZ, channels)


def padded_many(*grids):
    count = lax.axis_size("range")
    forward = [(i, i + 1) for i in range(count - 1)]
    backward = [(i + 1, i) for i in range(count - 1)]
    low = lax.ppermute(jnp.concatenate([g[:, :, PZ - 1 :] for g in grids], -1), "range", forward)
    high = lax.ppermute(jnp.concatenate([g[:, :, :1] for g in grids], -1), "range", backward)
    out = []
    for n, grid in enumerate(grids):
        width = grid.shape[-1]
        piece = slice(n * width, (n + 1) * width)
        wide = jnp.concatenate([low[..., piece], grid, high[..., piece]], axis=2)
        out.append(jnp.pad(wide, ((1, 1), (1, 1), (0, 0), (0, 0))))
    return out


def padded(grid):
    return padded_many(grid)[0]


def widened(depth, *grids):
    count = lax.axis_size("range")
    forward = [(i, i + 1) for i in range(count - 1)]
    backward = [(i + 1, i) for i in range(count - 1)]
    low = lax.ppermute(jnp.concatenate([g[:, :, PZ - depth :] for g in grids], -1), "range", forward)
    high = lax.ppermute(jnp.concatenate([g[:, :, :depth] for g in grids], -1), "range", backward)
    out = []
    for n, grid in enumerate(grids):
        width = grid.shape[-1]
        piece = slice(n * width, (n + 1) * width)
        out.append(jnp.concatenate([low[..., piece], grid, high[..., piece]], axis=2))
    return out


def xy_padded(grid):
    return jnp.pad(grid, ((1, 1), (1, 1), (0, 0), (0, 0)))


def z_columns_n(pad, planes):
    return jnp.concatenate([pad[:, :, sz : sz + planes] for sz in range(3)], axis=-1)


def z_columns_reversed(pad):
    return jnp.concatenate([pad[:, :, sz : sz + PZ] for sz in (2, 1, 0)], axis=-1)


def conv_apply_reversed(zcols, weights):
    channels = weights.shape[-1]
    taps = weights.transpose(0, 2, 1).reshape(3, 3, 3 * channels, channels)
    total = None
    for sx in range(3):
        for sy in range(3):
            term = jnp.dot(xy_window(zcols, sx, sy), taps[2 - sx, 2 - sy], preferred_element_type=jnp.float32)
            total = term if total is None else total + term
    return total


def z_columns(pad):
    return jnp.concatenate([pad[:, :, sz : sz + PZ] for sz in range(3)], axis=-1)


def xy_window(zcols, sx, sy):
    return zcols[sx : sx + 2 * PX, sy : sy + 2 * PY].reshape(-1, zcols.shape[-1])


def conv_apply(zcols, weights):
    channels = weights.shape[-1]
    taps = weights.reshape(3, 3, 3 * channels, channels)
    total = None
    for sx in range(3):
        for sy in range(3):
            term = jnp.dot(xy_window(zcols, sx, sy), taps[sx, sy], preferred_element_type=jnp.float32)
            total = term if total is None else total + term
    return total


def conv_weight_grad(zcols, upstream):
    contract_rows = (((0,), (0,)), ((), ()))
    terms = [
        lax.dot_general(xy_window(zcols, sx, sy), upstream, contract_rows, preferred_element_type=jnp.float32)
        for sx in range(3)
        for sy in range(3)
    ]
    return jnp.concatenate(terms, 0)

AXIS_SHIFT = {"y": 1, "x": 3, "z": 5}
PART_ORDERS = (("y", "x", "z"), ("x", "z", "y"), ("z", "y", "x"))


def coordinate(index, shift):
    return (index >> shift) & 3


def partner(index, shift, stage):
    c = (index >> shift) & 3
    other = c ^ 1 if stage == 0 else 3 - c
    return index + ((other - c) << shift)


def keep_bit(c, stage):
    if stage == 0:
        return ((c == 1) | (c == 2)).astype(jnp.int32)
    return (c >= 2).astype(jnp.int32)


def exchange_steps(order):
    return [(AXIS_SHIFT[axis], stage) for axis in order for stage in (0, 1)]


def split_halves(y, bit):
    h = y.shape[0] // 2
    keep = lax.dynamic_slice_in_dim(y, bit * h, h, 0)
    send = lax.dynamic_slice_in_dim(y, (1 - bit) * h, h, 0)
    return keep, send


def join_halves(y, got, bit):
    h = y.shape[0]
    full = jnp.zeros((2 * h,) + y.shape[1:], y.dtype)
    full = lax.dynamic_update_slice_in_dim(full, y, bit * h, 0)
    return lax.dynamic_update_slice_in_dim(full, got, (1 - bit) * h, 0)


def torus_psum(flat, late=(), later=()):
    count = lax.axis_size("range")
    index = lax.axis_index("range")
    core_perm = [(i, i ^ 1) for i in range(count)]
    core_bit = index & 1
    keep, send = split_halves(flat, core_bit)
    y = keep + lax.ppermute(send, "range", core_perm)
    y, late = lax.optimization_barrier((y, late))
    parts = jnp.split(y, len(PART_ORDERS), 0)
    reduced = []
    for part, order in zip(parts, PART_ORDERS):
        for shift, stage in exchange_steps(order[:1]):
            perm = [(i, partner(i, shift, stage)) for i in range(count)]
            bit = keep_bit(coordinate(index, shift), stage)
            keep, send = split_halves(part, bit)
            part = keep + lax.ppermute(send, "range", perm)
        for shift, stage in exchange_steps(order[1:]):
            perm = [(i, partner(i, shift, stage)) for i in range(count)]
            part = part + lax.ppermute(part, "range", perm)
        reduced.append(part)
    reduced, later = lax.optimization_barrier((reduced, later))
    gathered = []
    for part, order in zip(reduced, PART_ORDERS):
        part = part.astype(jnp.bfloat16)
        for shift, stage in reversed(exchange_steps(order[:1])):
            perm = [(i, partner(i, shift, stage)) for i in range(count)]
            bit = keep_bit(coordinate(index, shift), stage)
            part = join_halves(part, lax.ppermute(part, "range", perm), bit)
        gathered.append(part)
    y = jnp.concatenate(gathered, 0)
    return join_halves(y, lax.ppermute(y, "range", core_perm), core_bit).astype(jnp.float32), late, later


def reversed_kernel(weights):
    return jnp.flip(weights, 0).transpose(0, 2, 1)


def on_device(child_in, cotangent, child_of, neighbours, down_w, first_w, second_w):
    channels = child_in.shape[-1]
    kids_dev = child_in.shape[0]
    own_rank = lax.axis_index("range")
    f32 = jnp.float32
    bf16 = jnp.bfloat16

    slot_of = 2 * (neighbours[:, 4] >= 0).astype(jnp.int32) + (neighbours[:, 10] >= 0).astype(jnp.int32)
    match = slot_of[None, :] == jnp.arange(4, dtype=jnp.int32)[:, None]
    block_at = jnp.sum(jnp.where(match, jnp.arange(4, dtype=jnp.int32)[None, :], 0), axis=1)
    child_rows = child_of - own_rank * kids_dev
    fine_idx = child_rows[block_at].reshape(-1)
    inverse = jnp.zeros((kids_dev,), jnp.int32).at[fine_idx].set(jnp.arange(kids_dev, dtype=jnp.int32))

    fine = child_in[fine_idx].reshape(2, 2, 2, 2, 2, 2, 2, 2, 2, 4, 2, channels)
    patches = fine.transpose(0, 2, 5, 1, 3, 7, 4, 9, 6, 8, 10, 11).reshape(512, 8 * channels)
    down_flat = down_w.reshape(8 * channels, channels)
    hidden = jnp.dot(patches, down_flat, preferred_element_type=f32).astype(bf16)
    hidden_grid = hidden.reshape(2 * PX, 2 * PY, PZ, channels)

    cot_grid = to_grid(cotangent[block_at])
    cot_rows = cot_grid.reshape(-1, channels)
    hidden_wide, cot_wide = widened(2, hidden_grid, cot_grid)
    hidden_pad = xy_padded(hidden_wide)
    cot_pad = xy_padded(cot_wide)
    count = lax.axis_size("range")
    side_ok = jnp.stack([own_rank > 0, own_rank < count - 1]).reshape(2, 1, 1, 1)

    def halo_conv(pad, weights, reverse=False):
        order = (2, 1, 0) if reverse else (0, 1, 2)
        sides = [jnp.concatenate([pad[:, :, t + sz] for sz in order], -1) for t in (0, PZ + 1)]
        zc = jnp.stack(sides, 0)
        channels_out = weights.shape[-1]
        if reverse:
            taps = weights.transpose(0, 2, 1).reshape(3, 3, -1, channels_out)[::-1, ::-1]
        else:
            taps = weights.reshape(3, 3, -1, channels_out)
        total = None
        for sx in range(3):
            for sy in range(3):
                win = zc[:, sx : sx + 2 * PX, sy : sy + 2 * PY].reshape(-1, zc.shape[-1])
                term = jnp.dot(win, taps[sx, sy], preferred_element_type=f32)
                total = term if total is None else total + term
        return total.reshape(2, 2 * PX, 2 * PY, channels_out)

    def with_halo(own, halo):
        return jnp.concatenate([halo[0][:, :, None], own, halo[1][:, :, None]], axis=2)

    hidden_cols = z_columns(hidden_pad[:, :, 1 : PZ + 3])
    pre_act = conv_apply(hidden_cols, first_w)
    pre_halo = halo_conv(hidden_pad, first_w)
    act_own = jax.nn.silu(pre_act).astype(bf16).reshape(2 * PX, 2 * PY, PZ, channels)
    act_halo = jnp.where(side_ok, jax.nn.silu(pre_halo), 0.0).astype(bf16)
    act_cols = z_columns(xy_padded(with_halo(act_own, act_halo)))

    def d_pre_of(back, pre):
        sig = jax.nn.sigmoid(pre)
        return back * sig * (1.0 + pre * (1.0 - sig))

    cot_cols = z_columns_reversed(cot_pad[:, :, 1 : PZ + 3])
    back_act = conv_apply_reversed(cot_cols, second_w)
    back_halo = halo_conv(cot_pad, second_w, reverse=True)
    d_pre = d_pre_of(back_act, pre_act).astype(bf16)
    d_pre_halo = jnp.where(side_ok, d_pre_of(back_halo, pre_halo), 0.0).astype(bf16)
    d_pre_cols = z_columns_reversed(xy_padded(with_halo(d_pre.reshape(2 * PX, 2 * PY, PZ, channels), d_pre_halo)))
    d_hidden = (
        cot_rows.astype(f32)
        + conv_apply_reversed(d_pre_cols, first_w)
    ).astype(bf16)

    contract_rows = (((0,), (0,)), ((), ()))
    raw_first = conv_weight_grad(hidden_cols, d_pre)
    raw_second = conv_weight_grad(act_cols, cot_rows)
    raw_down = lax.dot_general(patches, d_hidden, contract_rows, preferred_element_type=f32)


    raw_grads = jnp.concatenate(
        [
            raw_down.reshape(8, channels, channels),
            raw_first.reshape(27, channels, channels),
            raw_second.reshape(27, channels, channels),
        ],
        0,
    )
    limit = jnp.float32(channels * math.sqrt(62.0))
    total_values = raw_grads.size
    rows = 8064
    flat = jnp.pad(raw_grads.reshape(-1), (0, rows * channels - total_values)).reshape(rows, channels)
    summed, (late_cols, late_hidden), late_d_hidden = torus_psum(flat, (act_cols, hidden), d_hidden)
    back = jnp.dot(late_d_hidden, down_flat.T, preferred_element_type=f32).astype(bf16)
    back = back.reshape(2, 2, 2, 2, 2, 2, 2, 4, 2, 2, 2, channels)
    back = back.transpose(0, 3, 1, 4, 6, 2, 8, 5, 9, 7, 10, 11).reshape(kids_dev, PX * PY * PZ, channels)
    child_grad = back[inverse]
    summed = summed.reshape(-1)[:total_values].reshape(raw_grads.shape)
    section = (late_hidden.astype(f32) + conv_apply(late_cols, second_w)).astype(bf16)
    partial = jnp.sum((summed * summed).reshape(summed.shape[0], -1), axis=1)
    grad_total = jnp.sqrt(jnp.sum(lax.optimization_barrier(partial)))
    clipped = summed * jnp.minimum(jnp.float32(1.0), limit / grad_total)
    section_out = from_grid(section.reshape(2 * PX, 2 * PY, PZ, channels))[slot_of]
    return (section_out, child_grad, clipped[:8], clipped[8:35], clipped[35:62])


def solution(mesh):
    in_specs = (
        P("range", None, None),
        P("range", None, None),
        P("range", None),
        P("range", None),
        P(),
        P(),
        P(),
    )
    out_specs = (P("range", None, None), P("range", None, None), P(), P(), P())
    return jax.shard_map(
        on_device, mesh=mesh, in_specs=in_specs, out_specs=out_specs, check_vma=False
    )
```
